256 devices in a mesh: depth: 4 (over y), tile: 64 (over x, z, core).
Axes of the slice: x: 4, y: 4, z: 8, core: 2. Of those that a mesh axis runs over, the one named last changes fastest.
Arguments:
- field: float32 [64, 256, 8192], P('depth', None, 'tile'), may hold values from -6 to 6
- light_vectors: float32 [16, 3], replicated, may hold values from -4 to 4
- transfer: float32 [16, 4, 8], replicated, may hold values from 0.05 to 1
- light_index: int32 [4], replicated, may hold values from 0 to 15
- flips: int32 [64], P('tile'), may hold values from 0 to 1
Outputs:
- frames: float32 [4, 4, 256, 8192], P(None, None, 'depth', 'tile')
The draws below stay inside these ranges and needn't reach their ends.
All inputs are finite; a program needn't handle non-finite values.
Results may differ from the reference program's by a relative error of at most 0.0003.
Values sent between devices are 32-bit elements; how exact they have to be, the bound alone decides.
A program may use at most 128 MiB of HBM per device.

```python
import jax
import jax.numpy as jnp
from jax import lax

BX = 128
BY = 256
PASSES = 4
LIGHTS = 16
KNOTS = 8
TILES = 64
NZ = 64
NX = 8192


def with_ends(values, key, least, top_value):
    index_at = [jax.random.randint(jax.random.fold_in(key, axis), (), 0, length) for axis, length in enumerate(values.shape)]
    main_axis = values.shape.index(max(values.shape))
    next_to = index_at[:main_axis] + [(index_at[main_axis] + 1) % values.shape[main_axis]] + index_at[main_axis + 1:]
    return values.at[tuple(index_at)].set(least).at[tuple(next_to)].set(top_value)


def levels(stream_key, shape, shards, least, largest):
    factor_of = 1.0
    for dim, blocks in shards:
        heights = jax.random.uniform(jax.random.fold_in(jax.random.fold_in(stream_key, 6), dim), (blocks,), jnp.float32, least / len(shards), largest / len(shards))
        factor_of = factor_of * jnp.repeat(jnp.exp(heights), shape[dim] // blocks).reshape((-1,) + (1,) * (len(shape) - 1 - dim))
    return factor_of


def bell_draw(own_key, shape, deviation, bound, split=(), kind=jnp.bfloat16):
    drawn = deviation * jax.random.normal(own_key, shape, jnp.float32)
    if split:
        drawn = drawn * levels(own_key, shape, split, -0.22, 0.18)
    return jnp.clip(drawn, -bound, bound).astype(kind)


def setup_inputs(seed: int = 0) -> dict:
    splits = jax.random.split(jax.random.key(seed), 6)
    field = bell_draw(splits[0], (NZ, BY, NX), 1.0, 6.0, ((0, 4), (2, 64)), jnp.float32)
    light_vectors = bell_draw(splits[1], (LIGHTS, 3), 1.0, 4.0, (), jnp.float32)
    transfer = jnp.clip(jax.random.uniform(splits[2], (LIGHTS, 4, KNOTS), jnp.float32, 0.05, 1.0), 0.05, 1.0)
    light_index = with_ends(jax.random.randint(splits[3], (PASSES,), 0, LIGHTS), jax.random.fold_in(splits[3], 1), 0, LIGHTS - 1).astype(jnp.int32)
    flips = with_ends(jax.random.randint(splits[4], (TILES,), 0, 2), jax.random.fold_in(splits[4], 1), 0, 1).astype(jnp.int32)
    return dict(field=field, light_vectors=light_vectors, transfer=transfer, light_index=light_index, flips=flips)


AMBIENT = 0.3

def shade_cells(values, grad_z, grad_y, grad_x, light_vec, curve, opacity_scale):
    knot_count = curve.shape[-1]
    position = jax.nn.sigmoid(values) * (knot_count - 1)
    mixed = [jnp.zeros_like(values) for channel in range(4)]
    for knot_index in range(knot_count):
        tent = jnp.maximum(0.0, 1.0 - jnp.abs(position - knot_index))
        mixed = [mixed[channel] + tent * curve[channel, knot_index] for channel in range(4)]
    facing = grad_x * light_vec[0] + grad_y * light_vec[1] + grad_z * light_vec[2]
    bright = AMBIENT + jnp.abs(facing) / jnp.sqrt(grad_x * grad_x + grad_y * grad_y + grad_z * grad_z + 1.0)
    opacity = mixed[3] * opacity_scale
    emitted = [mixed[channel] * bright * opacity for channel in range(3)]
    return (emitted, opacity)

def march(emitted, opacity, flip):
    log_keep = jnp.log1p(-opacity)
    running = jnp.cumsum(log_keep, axis=0)
    column_sum = running[-1]
    before = jnp.where(flip == 1, column_sum[None] - running, running - log_keep)
    carried = jnp.exp(before)
    colors = [lax.optimization_barrier(jnp.sum(carried * emitted[channel], axis=0)) for channel in range(3)]
    return jnp.stack(colors + [jnp.exp(column_sum)])

def reference(field, light_vectors, transfer, light_index, flips):
    scale = 2.0 / field.shape[0]
    padded = jnp.pad(field, ((1, 1), (1, 1), (1, 1)))

    def render_tile(tile_index):
        start = (tile_index * BX).astype(jnp.int32)
        block = lax.dynamic_slice_in_dim(padded, start, BX + 2, 2)
        center = block[1:-1, 1:-1, 1:-1]
        grad_z = (block[2:, 1:-1, 1:-1] - block[:-2, 1:-1, 1:-1]) * 0.5
        grad_y = (block[1:-1, 2:, 1:-1] - block[1:-1, :-2, 1:-1]) * 0.5
        grad_x = (block[1:-1, 1:-1, 2:] - block[1:-1, 1:-1, :-2]) * 0.5
        flip = flips[tile_index]
        images = []
        for pass_index in range(PASSES):
            chosen = light_index[pass_index]
            emitted, opacity = shade_cells(center, grad_z, grad_y, grad_x, light_vectors[chosen], transfer[chosen], scale)
            images.append(march(emitted, opacity, flip))
        return jnp.stack(images)
    tiled = lax.map(render_tile, jnp.arange(TILES, dtype=jnp.int32))
    images = jnp.transpose(tiled, (1, 2, 3, 0, 4)).reshape(PASSES, 4, BY, TILES * BX)
    return jnp.concatenate([images[:, :3], 1.0 - images[:, 3:]], axis=1)
```

```python
import functools

import jax
import jax.numpy as jnp
from jax import lax
from jax.experimental import pallas as pl
from jax.experimental.pallas import tpu as pltpu
from jax.sharding import PartitionSpec as P

PASSES = 4
CHANNELS = 4
KNOTS = 8
AMBIENT = 0.3
RANKS = 4
SUB = 8
LANES = 128
SLAB = 16
DEPTH = 64
ROWS = 64
CHUNKS = ROWS // SUB
HALF = SLAB // 2
STEP = 8
PACK = 48
WIDE = 3 * KNOTS * SUB
TALL = PASSES * CHANNELS * SUB
MESH = pl.DeviceIdType.MESH


def rows_at(start):
    return pl.ds(pl.multiple_of(start, SUB), SUB)


def build_weights(lights, transfer, weights):
    sub = lax.broadcasted_iota(jnp.int32, (SUB, KNOTS * SUB), 0)
    lane = lax.broadcasted_iota(jnp.int32, (SUB, KNOTS * SUB), 1)
    knot = lane // SUB
    diagonal = (lane % SUB) == sub
    high, low = [], []
    for p in range(PASSES):
        chosen = lights[p]
        for c in range(CHANNELS):
            line = jnp.zeros((SUB, KNOTS * SUB), jnp.float32)
            for k in range(KNOTS):
                line = jnp.where(knot == k, transfer[chosen, c, k], line)
            if c == CHANNELS - 1:
                line = line * (2.0 / DEPTH)
            line = jnp.where(diagonal, line, 0.0)
            top = line.astype(jnp.bfloat16).astype(jnp.float32)
            high.append(top)
            low.append(line - top)
    high = jnp.concatenate(high, axis=0)
    low = jnp.concatenate(low, axis=0)
    weights[...] = jnp.concatenate([high, low, high], axis=1).astype(jnp.bfloat16)


def pack_borders(tile, tiles, slab, pack, left, right):
    sub = lax.broadcasted_iota(jnp.int32, (SUB, LANES), 0)
    lane = lax.broadcasted_iota(jnp.int32, (SUB, LANES), 1)
    zero = jnp.zeros((SUB, LANES), jnp.float32)
    for rank in range(RANKS):
        base = rank * ROWS
        for part in range(SLAB // SUB):
            above, below = zero, zero
            for s in range(SUB):
                d = part * SUB + s
                if rank > 0:
                    line = slab[d, base - SUB : base, :]
                    above = jnp.where(sub == s, pltpu.roll(line, (s + 1) % SUB, 0), above)
                if rank < RANKS - 1:
                    line = slab[d, base + ROWS : base + ROWS + SUB, :]
                    below = jnp.where(sub == s, pltpu.roll(line, s, 0), below)
            pack[rank, part * SUB : (part + 1) * SUB, :] = above
            pack[rank, SLAB + part * SUB : SLAB + (part + 1) * SUB, :] = below

        def gather(d, carry):
            first, last = carry
            for c in range(CHUNKS):
                place = d * CHUNKS + c
                block = slab[d, base + c * SUB : base + (c + 1) * SUB, :]
                here = lane == place
                first = jnp.where(here, pltpu.roll(block, place, 1), first)
                last = jnp.where(here, pltpu.roll(block, lax.rem(place + 1, LANES), 1), last)
            return first, last

        first, last = lax.fori_loop(0, SLAB, gather, (zero, zero))
        left[rank] = jnp.where(tile == 0, 0.0, first)
        right[rank] = jnp.where(tile == tiles - 1, 0.0, last)


def prepare(chunk, volume, halo, place_ref, nx_ref, ny_ref, nz_ref):
    sub = lax.broadcasted_iota(jnp.int32, (SUB, LANES), 0)
    lane = lax.broadcasted_iota(jnp.int32, (SUB, LANES), 1)
    here = rows_at(SUB + SUB * chunk)
    above = rows_at(SUB * chunk)
    below = rows_at(2 * SUB + SUB * chunk)

    def cells(step, carry):
        for u in range(STEP):
            d = step * STEP + u
            slab = d // SLAB
            place = (d % SLAB) * CHUNKS + chunk
            x = volume[d + 1, here, :]
            dz = volume[d + 2, here, :] - volume[d, here, :]
            up = pltpu.roll(jnp.where(sub == SUB - 1, volume[d + 1, above, :], x), 1, 0)
            down = pltpu.roll(jnp.where(sub == 0, volume[d + 1, below, :], x), SUB - 1, 0)
            dy = down - up
            west = pltpu.roll(halo[slab, 32:40, :], LANES - 1 - place, 1)
            east = pltpu.roll(halo[slab, 40:48, :], lax.rem(LANES - place, LANES), 1)
            prior = pltpu.roll(jnp.where(lane == LANES - 1, west, x), 1, 1)
            after = pltpu.roll(jnp.where(lane == 0, east, x), LANES - 1, 1)
            dx = after - prior
            scale = lax.rsqrt(dx * dx + dy * dy + dz * dz + 4.0)
            nx_ref[d] = dx * scale
            ny_ref[d] = dy * scale
            nz_ref[d] = dz * scale
            place_ref[d] = 3.5 + 3.5 * jnp.tanh(0.5 * x)
        return carry

    lax.fori_loop(0, DEPTH // STEP, cells, 0)


def shade(flip, vectors, weights, place_ref, nx_ref, ny_ref, nz_ref, write):
    start = flip * (DEPTH - 1)
    sign = 1 - 2 * flip
    knots = jnp.concatenate(
        [jnp.full((SUB, LANES), float(k), jnp.float32) for k in range(KNOTS)], axis=0
    )

    def cells(step, state):
        state = list(state)
        at = [start + sign * (step * STEP + u) for u in range(STEP)]
        highs, lows = [], []
        for u in range(STEP):
            place = place_ref[at[u]]
            tent = jnp.maximum(
                0.0, 1.0 - jnp.abs(jnp.concatenate([place] * KNOTS, axis=0) - knots)
            )
            high = tent.astype(jnp.bfloat16)
            lows.append((tent - high.astype(jnp.float32)).astype(jnp.bfloat16))
            highs.append(high)
        for pair in range(STEP // 2):
            a, b = 2 * pair, 2 * pair + 1
            high = jnp.concatenate([highs[a], highs[b]], axis=1)
            low = jnp.concatenate([lows[a], lows[b]], axis=1)
            moving = jnp.concatenate([high, high, low], axis=0)
            mixed = jnp.dot(weights[...], moving, preferred_element_type=jnp.float32)
            for side in range(2):
                u = 2 * pair + side
                nx, ny, nz = nx_ref[at[u]], ny_ref[at[u]], nz_ref[at[u]]
                for p in range(PASSES):
                    channel = [
                        mixed[
                            (p * CHANNELS + c) * SUB : (p * CHANNELS + c + 1) * SUB,
                            side * LANES : (side + 1) * LANES,
                        ]
                        for c in range(CHANNELS)
                    ]
                    lx, ly, lz = vectors[p]
                    bright = AMBIENT + jnp.abs(nx * lx + ny * ly + nz * lz)
                    through = state[p * CHANNELS + 3]
                    taken = through * channel[3]
                    state[p * CHANNELS + 3] = through - taken
                    gain = taken * bright
                    for c in range(3):
                        state[p * CHANNELS + c] = state[p * CHANNELS + c] + gain * channel[c]
        return tuple(state)

    zero = jnp.zeros((SUB, LANES), jnp.float32)
    one = jnp.ones((SUB, LANES), jnp.float32)
    state = lax.fori_loop(
        0, DEPTH // STEP, cells, tuple([zero, zero, zero, one] * PASSES)
    )
    for p in range(PASSES):
        for c in range(3):
            write(p, c, state[p * CHANNELS + c])
        write(p, 3, 1.0 - state[p * CHANNELS + 3])


def kernel(
    tiles,
    flips, lights, light_vectors, transfer, field,
    out,
    slab, volume, pack, left, right, halo, relay, pack_relay, weights,
    place_ref, nx_ref, ny_ref, nz_ref,
    local_sem, col_send, col_recv, pack_send, pack_recv, pack_relay_recv, pack_forward,
    near_send, near_recv, far_send, far_recv, hop_send, hop_recv,
):
    rank = lax.axis_index("depth")
    tile = lax.axis_index("tile")
    ahead, behind = (rank + 1) % RANKS, (rank + RANKS - 1) % RANKS
    across = (rank + 2) % RANKS
    sides = (ahead, behind)
    east, west = (tile + 1) % tiles, (tile + tiles - 1) % tiles

    fetch = pltpu.make_async_copy(field, slab, local_sem.at[0])
    fetch.start()
    own = pltpu.make_async_copy(
        field.at[:, pl.ds(pl.multiple_of(rank * ROWS, SUB), ROWS), :],
        volume.at[pl.ds(1 + rank * SLAB, SLAB), pl.ds(SUB, ROWS), :],
        local_sem.at[1],
    )
    own.start()

    barrier = pltpu.get_barrier_semaphore()
    for where in sides:
        pl.semaphore_signal(barrier, inc=1, device_id=(where, tile), device_id_type=MESH)
    for where in (east, west):
        pl.semaphore_signal(barrier, inc=1, device_id=(rank, where), device_id_type=MESH)
    pl.semaphore_wait(barrier, 4)

    def near(side, c):
        return pltpu.make_async_remote_copy(
            src_ref=field.at[:, rows_at(sides[side] * ROWS + c * SUB), :],
            dst_ref=volume.at[pl.ds(1 + rank * SLAB, SLAB), rows_at(SUB + c * SUB), :],
            send_sem=near_send.at[side, c],
            recv_sem=near_recv.at[side, c],
            device_id=(sides[side], tile),
            device_id_type=MESH,
        )

    def far(side, c):
        return pltpu.make_async_remote_copy(
            src_ref=field.at[pl.ds(side * HALF, HALF), rows_at(across * ROWS + c * SUB), :],
            dst_ref=relay.at[side, c],
            send_sem=far_send.at[side, c],
            recv_sem=far_recv.at[side, c],
            device_id=(sides[side], tile),
            device_id_type=MESH,
        )

    def hop(side, c):
        origin = sides[1 - side]
        return pltpu.make_async_remote_copy(
            src_ref=relay.at[side, c],
            dst_ref=volume.at[
                pl.ds(1 + origin * SLAB + side * HALF, HALF), rows_at(SUB + c * SUB), :
            ],
            send_sem=hop_send.at[side, c],
            recv_sem=hop_recv.at[side, c],
            device_id=(sides[side], tile),
            device_id_type=MESH,
        )

    for side in range(2):
        far(side, 0).start()
    for side in range(2):
        far(side, 1).start()
    for side in range(2):
        near(side, 0).start()

    zero_layer = jnp.zeros((ROWS + 2 * SUB, LANES), jnp.float32)
    volume[0] = zero_layer
    volume[DEPTH + 1] = zero_layer
    fetch.wait()
    pack_borders(tile, tiles, slab, pack, left, right)
    build_weights(lights, transfer, weights)

    columns = [
        pltpu.make_async_remote_copy(
            src_ref=source,
            dst_ref=pack.at[:, pl.ds(start, SUB), :],
            send_sem=col_send.at[n],
            recv_sem=col_recv.at[n],
            device_id=(rank, where),
            device_id_type=MESH,
        )
        for n, (source, start, where) in enumerate(((right, 32, east), (left, 40, west)))
    ]
    for copy in columns:
        copy.start()
    own.wait()
    for copy in columns:
        copy.wait_recv()

    packs = [
        pltpu.make_async_remote_copy(
            src_ref=pack.at[sides[side]],
            dst_ref=halo.at[rank],
            send_sem=pack_send.at[side],
            recv_sem=pack_recv.at[side],
            device_id=(sides[side], tile),
            device_id_type=MESH,
        )
        for side in range(2)
    ]
    packs.append(
        pltpu.make_async_remote_copy(
            src_ref=pack.at[across],
            dst_ref=pack_relay,
            send_sem=pack_send.at[2],
            recv_sem=pack_relay_recv,
            device_id=(ahead, tile),
            device_id_type=MESH,
        )
    )
    packs[2].start()
    packs[0].start()
    packs[1].start()
    mine = pltpu.make_async_copy(pack.at[rank], halo.at[rank], local_sem.at[2])
    mine.start()
    packs[2].wait_recv()
    forward = pltpu.make_async_remote_copy(
        src_ref=pack_relay,
        dst_ref=halo.at[behind],
        send_sem=pack_forward.at[0],
        recv_sem=pack_forward.at[1],
        device_id=(ahead, tile),
        device_id_type=MESH,
    )
    forward.start()
    mine.wait()
    packs[0].wait_recv()
    packs[1].wait_recv()
    forward.wait_recv()

    def expand(d, carry):
        source = d // SLAB
        line = d % SLAB
        volume[d + 1, 0:SUB, :] = jnp.broadcast_to(halo[source, pl.ds(line, 1), :], (SUB, LANES))
        volume[d + 1, SUB + ROWS : ROWS + 2 * SUB, :] = jnp.broadcast_to(
            halo[source, pl.ds(SLAB + line, 1), :], (SUB, LANES)
        )
        return carry

    lax.fori_loop(0, DEPTH, expand, 0)

    flip = flips[0]
    vectors = [[light_vectors[lights[p], a] for a in range(3)] for p in range(PASSES)]

    def compute(chunk):
        prepare(chunk, volume, halo, place_ref, nx_ref, ny_ref, nz_ref)

        def write(p, c, value):
            out[p, c, rows_at(chunk * SUB), :] = value

        shade(flip, vectors, weights, place_ref, nx_ref, ny_ref, nz_ref, write)

    def advance(c, carry):
        @pl.when(c < CHUNKS)
        def _():
            for side in range(2):
                far(side, c).wait_recv()
                hop(side, c).start()

        @pl.when(c < CHUNKS - 2)
        def _():
            for side in range(2):
                far(side, c + 2).start()

        @pl.when(c < CHUNKS - 1)
        def _():
            for side in range(2):
                near(side, c + 1).start()

        @pl.when(c < CHUNKS)
        def _():
            for side in range(2):
                near(side, c).wait_recv()
                hop(side, c).wait_recv()

        @pl.when(c > 0)
        def _():
            compute(c - 1)

        return carry

    lax.fori_loop(0, CHUNKS + 1, advance, 0)

    def drain(c, carry):
        for side in range(2):
            near(side, c).wait_send()
            far(side, c).wait_send()
            hop(side, c).wait_send()
        return carry

    lax.fori_loop(0, CHUNKS, drain, 0)
    for copy in columns + packs + [forward]:
        copy.wait_send()


def solution(mesh):
    tiles = mesh.shape["tile"]

    def on_device(field, light_vectors, transfer, light_index, flips):
        smem = pl.BlockSpec(memory_space=pltpu.SMEM)
        vmem = pl.BlockSpec(memory_space=pltpu.VMEM)
        dma = pltpu.SemaphoreType.DMA
        f32 = jnp.float32
        return pl.pallas_call(
            functools.partial(kernel, tiles),
            out_shape=jax.ShapeDtypeStruct((PASSES, CHANNELS, ROWS, LANES), f32),
            in_specs=[smem, smem, smem, smem, pl.BlockSpec(memory_space=pl.ANY)],
            out_specs=vmem,
            scratch_shapes=[
                pltpu.VMEM((SLAB, RANKS * ROWS, LANES), f32),
                pltpu.VMEM((DEPTH + 2, ROWS + 2 * SUB, LANES), f32),
                pltpu.VMEM((RANKS, PACK, LANES), f32),
                pltpu.VMEM((RANKS, SUB, LANES), f32),
                pltpu.VMEM((RANKS, SUB, LANES), f32),
                pltpu.VMEM((RANKS, PACK, LANES), f32),
                pltpu.VMEM((2, CHUNKS, HALF, SUB, LANES), f32),
                pltpu.VMEM((PACK, LANES), f32),
                pltpu.VMEM((TALL, WIDE), jnp.bfloat16),
                pltpu.VMEM((DEPTH, SUB, LANES), f32),
                pltpu.VMEM((DEPTH, SUB, LANES), f32),
                pltpu.VMEM((DEPTH, SUB, LANES), f32),
                pltpu.VMEM((DEPTH, SUB, LANES), f32),
                dma((3,)), dma((2,)), dma((2,)), dma((3,)), dma((2,)), dma, dma((2,)),
                dma((2, CHUNKS)), dma((2, CHUNKS)), dma((2, CHUNKS)),
                dma((2, CHUNKS)), dma((2, CHUNKS)), dma((2, CHUNKS)),
            ],
            compiler_params=pltpu.CompilerParams(collective_id=0, has_side_effects=True),
            name="render",
        )(flips, light_index, light_vectors, transfer, field)

    in_specs = (P("depth", None, "tile"), P(), P(), P(), P("tile"))
    out_specs = P(None, None, "depth", "tile")
    return jax.shard_map(
        on_device, mesh=mesh, in_specs=in_specs, out_specs=out_specs, check_vma=False
    )
```

```python
import functools

import jax
import jax.numpy as jnp
from jax import lax
from jax.experimental import pallas as pl
from jax.experimental.pallas import tpu as pltpu
from jax.sharding import PartitionSpec as P

PASSES = 4
CHANNELS = 4
KNOTS = 8
AMBIENT = 0.3
RANKS = 4
SUB = 8
LANES = 128
SLAB = 16
DEPTH = 64
ROWS = 64
CHUNKS = ROWS // SUB
HALF = SLAB // 2
STEP = 64
PACK = 48
TWO = 2 * SUB
FINE = 32.0
SPAN = 0.5 * (KNOTS - 1) * FINE
SLOTS = KNOTS - 1 + 3
OUTPUTS = CHANNELS + 1
WIDE = (3 * SLOTS + 2) * SUB
TALL = PASSES * OUTPUTS * SUB
STAGED = 4
MESH = pl.DeviceIdType.MESH


def rows_at(start):
    return pl.ds(pl.multiple_of(start, SUB), SUB)


def build_weights(lights, vectors, transfer, weights):
    sub = lax.broadcasted_iota(jnp.int32, (SUB, WIDE), 0)
    lane = lax.broadcasted_iota(jnp.int32, (SUB, WIDE), 1)
    slot = lane // SUB
    diagonal = (lane % SUB) == sub
    constant = slot >= 3 * SLOTS
    item = jnp.where(constant, SLOTS, slot % SLOTS)
    is_low = ((slot >= SLOTS) & (slot < 2 * SLOTS)) | (slot == 3 * SLOTS + 1)
    for p in range(PASSES):
        chosen = lights[p]
        for c in range(OUTPUTS):
            line = jnp.zeros((SUB, WIDE), jnp.float32)
            if c < CHANNELS:
                scale = 2.0 / DEPTH if c == CHANNELS - 1 else 1.0
                values = [transfer[c, k, chosen] * scale for k in range(KNOTS)]
                for k in range(KNOTS - 1):
                    line = jnp.where(item == k, (values[k + 1] - values[k]) * (1.0 / FINE), line)
                line = jnp.where(item == SLOTS, values[0], line)
            else:
                for n, axis in enumerate((2, 0, 1)):
                    line = jnp.where(item == KNOTS - 1 + n, vectors[axis, chosen], line)
            line = jnp.where(diagonal, line, 0.0)
            high = line.astype(jnp.bfloat16).astype(jnp.float32)
            start = (p * OUTPUTS + c) * SUB
            staged = jnp.where(is_low, line - high, high)
            weights[start : start + SUB, :] = staged


def pack_borders(tile, tiles, slab, pack, left, right):
    sub = lax.broadcasted_iota(jnp.int32, (SUB, LANES), 0)
    lane = lax.broadcasted_iota(jnp.int32, (SUB, LANES), 1)
    zero = jnp.zeros((SUB, LANES), jnp.float32)

    def gather(rank, carry):
        base = rank * ROWS
        first, last = [zero] * 2, [zero] * 2
        for d in range(SLAB):
            for c in range(CHUNKS):
                place = d * CHUNKS + c
                block = slab[d, pl.ds(pl.multiple_of(base + c * SUB, SUB), SUB), :]
                here = lane == place
                first[c % 2] = jnp.where(here, pltpu.roll(block, place, 1) if place else block, first[c % 2])
                last[c % 2] = jnp.where(here, pltpu.roll(block, place + 1, 1) if place < LANES - 1 else block, last[c % 2])
        left[rank] = jnp.where(tile == 0, 0.0, first[0] + first[1])
        right[rank] = jnp.where(tile == tiles - 1, 0.0, last[0] + last[1])
        return carry

    lax.fori_loop(0, RANKS, gather, 0)
    for rank in range(RANKS):
        base = rank * ROWS
        for part in range(SLAB // SUB):
            above, below = zero, zero
            for s in range(SUB):
                d = part * SUB + s
                if rank > 0:
                    line = slab[d, base - SUB : base, :]
                    above = jnp.where(sub == s, pltpu.roll(line, (s + 1) % SUB, 0), above)
                if rank < RANKS - 1:
                    line = slab[d, base + ROWS : base + ROWS + SUB, :]
                    below = jnp.where(sub == s, pltpu.roll(line, s, 0), below)
            pack[rank, part * SUB : (part + 1) * SUB, :] = above
            pack[rank, SLAB + part * SUB : SLAB + (part + 1) * SUB, :] = below


def pair(a, b):
    return jnp.concatenate([a, b], axis=0).astype(jnp.float32).astype(jnp.bfloat16)


def build_shift(shift):
    lane = lax.broadcasted_iota(jnp.int32, (LANES, LANES), 0)
    out = lax.broadcasted_iota(jnp.int32, (LANES, LANES), 1)
    inner = jnp.where(lane == out + 1, 1.0, jnp.where(lane == out - 1, -1.0, 0.0))
    place = lane % CHUNKS
    outer = jnp.where(
        (out == LANES - 1) & (place == 0), 1.0, jnp.where((out == 0) & (place == 1), -1.0, 0.0)
    )
    for n, part in enumerate((inner, inner, outer, outer)):
        shift[n * LANES : (n + 1) * LANES, :] = part.astype(jnp.bfloat16)


def prepare(chunk, volume, halo, shift, stage):
    lane = lax.broadcasted_iota(jnp.int32, (SUB, LANES), 1)
    bf16 = jnp.bfloat16
    first = lane % CHUNKS == 0
    couple = pair(lane // 2, lane // 2)
    nothing = jnp.zeros((TWO, LANES), bf16)
    here = rows_at(SUB + SUB * chunk)
    above = pl.ds(SUB + SUB * chunk - 1, SUB)
    below = pl.ds(SUB + SUB * chunk + 1, SUB)
    for source in range(RANKS):
        west = pltpu.roll(halo[source, 32:40, :], (LANES + 1 - chunk) % LANES, 1)
        east = pltpu.roll(halo[source, 40:48, :], (LANES - chunk) % LANES, 1)
        border = jnp.where(first, east, west)
        border_top = pair(border, border)
        rest = border - border_top[:SUB].astype(jnp.float32)
        border_low = pair(rest, rest)
        rows = []
        for two in range(SLAB // 2):
            d = source * SLAB + 2 * two
            x = jnp.concatenate([volume[d + 1, here, :], volume[d + 2, here, :]], axis=0)
            top = x.astype(bf16)
            low = (x - top.astype(jnp.float32)).astype(bf16)
            wanted = jnp.concatenate(
                [jnp.full((SUB, LANES), float((2 * two + n) * CHUNKS // 2), jnp.float32) for n in range(2)],
                axis=0,
            ).astype(bf16)
            mask = couple == wanted
            rows.append(
                jnp.concatenate(
                    [top, low, jnp.where(mask, border_top, nothing), jnp.where(mask, border_low, nothing)],
                    axis=1,
                )
            )
        across = jnp.dot(
            jnp.concatenate(rows, axis=0), shift[...], preferred_element_type=jnp.float32
        )
        for u in range(SLAB):
            d = source * SLAB + u
            dx = across[u * SUB : (u + 1) * SUB, :]
            dz = volume[d + 2, here, :] - volume[d, here, :]
            dy = volume[d + 1, below, :] - volume[d + 1, above, :]
            scale = lax.rsqrt(dx * dx + dy * dy + dz * dz + 4.0)
            stage[d, 0] = SPAN + SPAN * jnp.tanh(0.5 * volume[d + 1, here, :])
            stage[d, 1] = dx * scale
            stage[d, 2] = dy * scale
            stage[d, 3] = dz * scale


def shade(flip, weights, stage, write):
    start = flip * (DEPTH - 1)
    sign = 1 - 2 * flip
    bf16 = jnp.bfloat16

    def levels(values):
        return jnp.concatenate([jnp.full((SUB, LANES), float(v), jnp.float32) for v in values], axis=0).astype(bf16)

    none = jnp.zeros((SUB, LANES), jnp.float32)
    fine_ones = jnp.full((SUB, LANES), FINE, jnp.float32)
    base = [levels((FINE * 2 * n, FINE * (2 * n + 1))) for n in range(4)]
    index = [levels((2 * n, 2 * n + 1 if n < 3 else 99)) for n in range(4)]
    zero2 = levels((0, 0))
    full2 = levels((FINE, FINE))
    ones = levels((1, 1))

    def cells(step, state):
        state = list(state)
        columns = []
        for u in range(STEP):
            at = start + sign * (step * STEP + u)
            place, nx, ny, nz = [stage[at, n] for n in range(STAGED)]
            level = jnp.floor(place)
            step_in = place - level
            floor_knot = jnp.floor(level * (1.0 / FINE))
            whole, rest, knot = pair(level, level), pair(step_in, step_in), pair(floor_knot, floor_knot)
            flat, deep, deep_full = pair(nx, ny), pair(none, nz), pair(fine_ones, nz)
            flat_top, deep_top = flat.astype(jnp.float32), deep.astype(jnp.float32)
            flat_low = pair(nx - flat_top[:SUB], ny - flat_top[SUB:])
            deep_low = pair(none, nz - deep_top[SUB:])
            ramp = [
                jnp.minimum(
                    jnp.maximum(whole - base[n], zero2 if n < 3 else deep),
                    full2 if n < 3 else deep_full,
                )
                for n in range(4)
            ]
            fine = [
                jnp.where(knot == index[n], rest, zero2 if n < 3 else deep_low) for n in range(4)
            ]
            top = ramp + [flat]
            columns.append(jnp.concatenate(top + top + fine + [flat_low, ones], axis=0))
        for two in range(STEP // 2):
            moving = jnp.concatenate(columns[2 * two : 2 * two + 2], axis=1)
            mixed = jnp.dot(weights[...], moving, preferred_element_type=jnp.float32)
            for side in range(2):
                for p in range(PASSES):
                    red, green, blue, opacity, facing = [
                        mixed[
                            (p * OUTPUTS + c) * SUB : (p * OUTPUTS + c + 1) * SUB,
                            side * LANES : (side + 1) * LANES,
                        ]
                        for c in range(OUTPUTS)
                    ]
                    bright = AMBIENT + jnp.abs(facing)
                    through = state[p * CHANNELS + 3]
                    taken = through * opacity
                    state[p * CHANNELS + 3] = through - taken
                    gain = taken * bright
                    for c, channel in enumerate((red, green, blue)):
                        state[p * CHANNELS + c] = state[p * CHANNELS + c] + gain * channel
        return tuple(state)

    zero = jnp.zeros((SUB, LANES), jnp.float32)
    one = jnp.ones((SUB, LANES), jnp.float32)
    state = cells(0, tuple([zero, zero, zero, one] * PASSES))
    for p in range(PASSES):
        for c in range(3):
            write(p, c, state[p * CHANNELS + c])
        write(p, 3, 1.0 - state[p * CHANNELS + 3])


def kernel(
    tiles,
    flips, lights, light_vectors, transfer, field,
    out,
    slab, volume, pack, left, right, halo, relay, pack_relay, draft, weights, shift, stage,
    local_sem, col_send, col_recv, pack_send, pack_recv, pack_relay_recv, pack_forward,
    near_send, near_recv, far_send, far_recv, hop_send, hop_recv,
):
    rank = lax.axis_index("depth")
    tile = lax.axis_index("tile")
    ahead, behind = (rank + 1) % RANKS, (rank + RANKS - 1) % RANKS
    across = (rank + 2) % RANKS
    sides = (ahead, behind)
    east, west = (tile + 1) % tiles, (tile + tiles - 1) % tiles

    fetch = pltpu.make_async_copy(field, slab, local_sem.at[0])
    fetch.start()
    own = pltpu.make_async_copy(
        field.at[:, pl.ds(pl.multiple_of(rank * ROWS, SUB), ROWS), :],
        volume.at[pl.ds(1 + rank * SLAB, SLAB), pl.ds(SUB, ROWS), :],
        local_sem.at[1],
    )
    own.start()

    barrier = pltpu.get_barrier_semaphore()
    for where in sides:
        pl.semaphore_signal(barrier, inc=1, device_id=(where, tile), device_id_type=MESH)
    for where in (east, west):
        pl.semaphore_signal(barrier, inc=1, device_id=(rank, where), device_id_type=MESH)
    pl.semaphore_wait(barrier, 4)

    def near(side, c):
        return pltpu.make_async_remote_copy(
            src_ref=field.at[:, rows_at(sides[side] * ROWS + c * SUB), :],
            dst_ref=volume.at[pl.ds(1 + rank * SLAB, SLAB), rows_at(SUB + c * SUB), :],
            send_sem=near_send.at[side, c],
            recv_sem=near_recv.at[side, c],
            device_id=(sides[side], tile),
            device_id_type=MESH,
        )

    def far(side, c):
        return pltpu.make_async_remote_copy(
            src_ref=field.at[pl.ds(side * HALF, HALF), rows_at(across * ROWS + c * SUB), :],
            dst_ref=relay.at[side, c],
            send_sem=far_send.at[side, c],
            recv_sem=far_recv.at[side, c],
            device_id=(sides[side], tile),
            device_id_type=MESH,
        )

    def hop(side, c):
        origin = sides[1 - side]
        return pltpu.make_async_remote_copy(
            src_ref=relay.at[side, c],
            dst_ref=volume.at[
                pl.ds(1 + origin * SLAB + side * HALF, HALF), rows_at(SUB + c * SUB), :
            ],
            send_sem=hop_send.at[side, c],
            recv_sem=hop_recv.at[side, c],
            device_id=(sides[side], tile),
            device_id_type=MESH,
        )

    def launch(c, carry):
        for side in range(2):
            far(side, c).start()
        return carry

    lax.fori_loop(0, CHUNKS, launch, 0)
    for side in range(2):
        near(side, 0).start()

    zero_layer = jnp.zeros((ROWS + 2 * SUB, LANES), jnp.float32)
    volume[0] = zero_layer
    volume[DEPTH + 1] = zero_layer
    fetch.wait()
    pack_borders(tile, tiles, slab, pack, left, right)
    build_weights(lights, light_vectors, transfer, draft)
    weights[...] = draft[...].astype(jnp.bfloat16)
    build_shift(shift)

    columns = [
        pltpu.make_async_remote_copy(
            src_ref=source,
            dst_ref=pack.at[:, pl.ds(start, SUB), :],
            send_sem=col_send.at[n],
            recv_sem=col_recv.at[n],
            device_id=(rank, where),
            device_id_type=MESH,
        )
        for n, (source, start, where) in enumerate(((right, 32, east), (left, 40, west)))
    ]
    for copy in columns:
        copy.start()
    own.wait()
    for copy in columns:
        copy.wait_recv()

    packs = [
        pltpu.make_async_remote_copy(
            src_ref=pack.at[sides[side]],
            dst_ref=halo.at[rank],
            send_sem=pack_send.at[side],
            recv_sem=pack_recv.at[side],
            device_id=(sides[side], tile),
            device_id_type=MESH,
        )
        for side in range(2)
    ]
    packs.append(
        pltpu.make_async_remote_copy(
            src_ref=pack.at[across],
            dst_ref=pack_relay,
            send_sem=pack_send.at[2],
            recv_sem=pack_relay_recv,
            device_id=(ahead, tile),
            device_id_type=MESH,
        )
    )
    packs[2].start()
    packs[0].start()
    packs[1].start()
    mine = pltpu.make_async_copy(pack.at[rank], halo.at[rank], local_sem.at[2])
    mine.start()
    packs[2].wait_recv()
    forward = pltpu.make_async_remote_copy(
        src_ref=pack_relay,
        dst_ref=halo.at[behind],
        send_sem=pack_forward.at[0],
        recv_sem=pack_forward.at[1],
        device_id=(ahead, tile),
        device_id_type=MESH,
    )
    forward.start()
    mine.wait()
    packs[0].wait_recv()
    packs[1].wait_recv()
    forward.wait_recv()

    def expand(d, carry):
        source = d // SLAB
        line = d % SLAB
        volume[d + 1, 0:SUB, :] = jnp.broadcast_to(halo[source, pl.ds(line, 1), :], (SUB, LANES))
        volume[d + 1, SUB + ROWS : ROWS + 2 * SUB, :] = jnp.broadcast_to(
            halo[source, pl.ds(SLAB + line, 1), :], (SUB, LANES)
        )
        return carry

    lax.fori_loop(0, DEPTH, expand, 0)

    flip = flips[0]

    def compute(chunk):
        prepare(chunk, volume, halo, shift, stage)

        def write(p, c, value):
            out[p, c, rows_at(chunk * SUB), :] = value

        shade(flip, weights, stage, write)

    def relay_on(c):
        for side in range(2):
            far(side, c).wait_recv()
            hop(side, c).start()

    relay_on(0)
    relay_on(1)
    for side in range(2):
        near(side, 1).start()

    def advance(c, carry):
        @pl.when(c < CHUNKS - 2)
        def _():
            relay_on(c + 2)
            for side in range(2):
                near(side, c + 2).start()

        @pl.when(c < CHUNKS)
        def _():
            for side in range(2):
                near(side, c).wait_recv()
                hop(side, c).wait_recv()

        @pl.when(c > 0)
        def _():
            compute(c - 1)

        return carry

    lax.fori_loop(0, CHUNKS + 1, advance, 0)

    def drain(c, carry):
        for side in range(2):
            near(side, c).wait_send()
            far(side, c).wait_send()
            hop(side, c).wait_send()
        return carry

    lax.fori_loop(0, CHUNKS, drain, 0)
    for copy in columns + packs + [forward]:
        copy.wait_send()


def solution(mesh):
    tiles = mesh.shape["tile"]

    def on_device(field, light_vectors, transfer, light_index, flips):
        smem = pl.BlockSpec(memory_space=pltpu.SMEM)
        vmem = pl.BlockSpec(memory_space=pltpu.VMEM)
        dma = pltpu.SemaphoreType.DMA
        f32 = jnp.float32
        return pl.pallas_call(
            functools.partial(kernel, tiles),
            out_shape=jax.ShapeDtypeStruct((PASSES, CHANNELS, ROWS, LANES), f32),
            in_specs=[smem, smem, smem, smem, pl.BlockSpec(memory_space=pl.ANY)],
            out_specs=vmem,
            scratch_shapes=[
                pltpu.VMEM((SLAB, RANKS * ROWS, LANES), f32),
                pltpu.VMEM((DEPTH + 2, ROWS + 2 * SUB, LANES), f32),
                pltpu.VMEM((RANKS, PACK, LANES), f32),
                pltpu.VMEM((RANKS, SUB, LANES), f32),
                pltpu.VMEM((RANKS, SUB, LANES), f32),
                pltpu.VMEM((RANKS, PACK, LANES), f32),
                pltpu.VMEM((2, CHUNKS, HALF, SUB, LANES), f32),
                pltpu.VMEM((PACK, LANES), f32),
                pltpu.VMEM((TALL, WIDE), f32),
                pltpu.VMEM((TALL, WIDE), jnp.bfloat16),
                pltpu.VMEM((4 * LANES, LANES), jnp.bfloat16),
                pltpu.VMEM((DEPTH, STAGED, SUB, LANES), f32),
                dma((3,)), dma((2,)), dma((2,)), dma((3,)), dma((2,)), dma, dma((2,)),
                dma((2, CHUNKS)), dma((2, CHUNKS)), dma((2, CHUNKS)),
                dma((2, CHUNKS)), dma((2, CHUNKS)), dma((2, CHUNKS)),
            ],
            compiler_params=pltpu.CompilerParams(collective_id=0, has_side_effects=True),
            name="render",
        )(flips, light_index, light_vectors.T, jnp.transpose(transfer, (1, 2, 0)), field)

    in_specs = (P("depth", None, "tile"), P(), P(), P(), P("tile"))
    out_specs = P(None, None, "depth", "tile")
    return jax.shard_map(
        on_device, mesh=mesh, in_specs=in_specs, out_specs=out_specs, check_vma=False
    )
```

```python
import functools

import jax
import jax.numpy as jnp
from jax import lax
from jax.experimental import pallas as pl
from jax.experimental.pallas import tpu as pltpu
from jax.sharding import PartitionSpec as P

PASSES = 4
CHANNELS = 4
KNOTS = 8
AMBIENT = 0.3
RANKS = 4
SUB = 8
LANES = 128
SLAB = 16
DEPTH = 64
ROWS = 64
CHUNKS = ROWS // SUB
HALF = SLAB // 2
STEP = 64
PACK = 64
LAST = CHUNKS - 1
MIDDLE = 48
TOTAL = ROWS + 3 * SUB
TWO = 2 * SUB
FINE = 32.0
SPAN = 0.5 * (KNOTS - 1) * FINE
SLOTS = KNOTS - 1 + 3
OUTPUTS = CHANNELS + 1
WIDE = (3 * SLOTS + 2) * SUB
TALL = PASSES * OUTPUTS * SUB
STAGED = 4
ORDER = ((("far", 0), ("far", 1), ("far", 2), ("far", 3), ("far", 4), ("far", 5), ("far", 6), ("far", 7), ("near", 0), ), (("hop", 0), ("hop", 1), ), (("hop", 2), ), (("near", 1), ("near", 2), ))
HOPS = sum(kind == "hop" for part in ORDER for kind, _ in part)
NEARS = sum(kind == "near" for part in ORDER for kind, _ in part)
MESH = pl.DeviceIdType.MESH


def rows_at(start):
    return pl.ds(pl.multiple_of(start, SUB), SUB)


def place_of(chunk):
    return pl.multiple_of(SUB * (1 + chunk + chunk // LAST), SUB)


def build_weights(lights, vectors, transfer, weights):
    sub = lax.broadcasted_iota(jnp.int32, (SUB, WIDE), 0)
    lane = lax.broadcasted_iota(jnp.int32, (SUB, WIDE), 1)
    slot = lane // SUB
    diagonal = (lane % SUB) == sub
    constant = slot >= 3 * SLOTS
    item = jnp.where(constant, SLOTS, slot % SLOTS)
    is_low = ((slot >= SLOTS) & (slot < 2 * SLOTS)) | (slot == 3 * SLOTS + 1)
    for p in range(PASSES):
        chosen = lights[p]
        for c in range(OUTPUTS):
            line = jnp.zeros((SUB, WIDE), jnp.float32)
            if c < CHANNELS:
                scale = 2.0 / DEPTH if c == CHANNELS - 1 else 1.0
                values = [transfer[c, k, chosen] * scale for k in range(KNOTS)]
                for k in range(KNOTS - 1):
                    line = jnp.where(item == k, (values[k + 1] - values[k]) * (1.0 / FINE), line)
                line = jnp.where(item == SLOTS, values[0], line)
            else:
                for n, axis in enumerate((2, 0, 1)):
                    line = jnp.where(item == KNOTS - 1 + n, vectors[axis, chosen], line)
            line = jnp.where(diagonal, line, 0.0)
            high = line.astype(jnp.bfloat16).astype(jnp.float32)
            start = (p * OUTPUTS + c) * SUB
            staged = jnp.where(is_low, line - high, high)
            weights[start : start + SUB, :] = staged


def pack_borders(tile, tiles, slab, pack, left, right):
    sub = lax.broadcasted_iota(jnp.int32, (SUB, LANES), 0)
    lane = lax.broadcasted_iota(jnp.int32, (SUB, LANES), 1)
    zero = jnp.zeros((SUB, LANES), jnp.float32)

    def gather(rank, carry):
        base = rank * ROWS
        first, last = [zero] * 2, [zero] * 2
        for d in range(SLAB):
            for c in range(CHUNKS):
                place = d * CHUNKS + c
                block = slab[d, pl.ds(pl.multiple_of(base + c * SUB, SUB), SUB), :]
                here = lane == place
                first[c % 2] = jnp.where(here, pltpu.roll(block, place, 1) if place else block, first[c % 2])
                last[c % 2] = jnp.where(here, pltpu.roll(block, place + 1, 1) if place < LANES - 1 else block, last[c % 2])
        left[rank] = jnp.where(tile == 0, 0.0, first[0] + first[1])
        right[rank] = jnp.where(tile == tiles - 1, 0.0, last[0] + last[1])
        return carry

    lax.fori_loop(0, RANKS, gather, 0)
    for rank in range(RANKS):
        base = rank * ROWS
        for part in range(SLAB // SUB):
            above, below = zero, zero
            for s in range(SUB):
                d = part * SUB + s
                if rank > 0:
                    line = slab[d, base - SUB : base, :]
                    above = jnp.where(sub == s, pltpu.roll(line, (s + 1) % SUB, 0), above)
                if rank < RANKS - 1:
                    line = slab[d, base + ROWS : base + ROWS + SUB, :]
                    below = jnp.where(sub == s, pltpu.roll(line, s, 0), below)
            pack[rank, part * SUB : (part + 1) * SUB, :] = above
            pack[rank, SLAB + part * SUB : SLAB + (part + 1) * SUB, :] = below
            middle = zero
            for s in range(SUB):
                line = slab[part * SUB + s, base + LAST * SUB : base + ROWS, :]
                middle = jnp.where(sub == s, pltpu.roll(line, s, 0) if s else line, middle)
            start = MIDDLE + part * SUB
            pack[rank, start : start + SUB, :] = middle


def pair(a, b):
    return jnp.concatenate([a, b], axis=0).astype(jnp.float32).astype(jnp.bfloat16)


def build_shift(shift):
    lane = lax.broadcasted_iota(jnp.int32, (LANES, LANES), 0)
    out = lax.broadcasted_iota(jnp.int32, (LANES, LANES), 1)
    inner = jnp.where(lane == out + 1, 1.0, jnp.where(lane == out - 1, -1.0, 0.0))
    place = lane % CHUNKS
    outer = jnp.where(
        (out == LANES - 1) & (place == 0), 1.0, jnp.where((out == 0) & (place == 1), -1.0, 0.0)
    )
    for n, part in enumerate((inner, inner, outer, outer)):
        shift[n * LANES : (n + 1) * LANES, :] = part.astype(jnp.bfloat16)


def prepare(chunk, volume, halo, shift, stage):
    lane = lax.broadcasted_iota(jnp.int32, (SUB, LANES), 1)
    bf16 = jnp.bfloat16
    first = lane % CHUNKS == 0
    couple = pair(lane // 2, lane // 2)
    nothing = jnp.zeros((TWO, LANES), bf16)
    start = place_of(chunk)
    here = pl.ds(start, SUB)
    above = pl.ds(start - 1, SUB)
    below = pl.ds(start + 1, SUB)
    for source in range(RANKS):
        west = pltpu.roll(halo[source, 32:40, :], (LANES + 1 - chunk) % LANES, 1)
        east = pltpu.roll(halo[source, 40:48, :], (LANES - chunk) % LANES, 1)
        border = jnp.where(first, east, west)
        border_top = pair(border, border)
        rest = border - border_top[:SUB].astype(jnp.float32)
        border_low = pair(rest, rest)
        rows = []
        for two in range(SLAB // 2):
            d = source * SLAB + 2 * two
            x = jnp.concatenate([volume[d + 1, here, :], volume[d + 2, here, :]], axis=0)
            top = x.astype(bf16)
            low = (x - top.astype(jnp.float32)).astype(bf16)
            wanted = jnp.concatenate(
                [jnp.full((SUB, LANES), float((2 * two + n) * CHUNKS // 2), jnp.float32) for n in range(2)],
                axis=0,
            ).astype(bf16)
            mask = couple == wanted
            rows.append(
                jnp.concatenate(
                    [top, low, jnp.where(mask, border_top, nothing), jnp.where(mask, border_low, nothing)],
                    axis=1,
                )
            )
        across = jnp.dot(
            jnp.concatenate(rows, axis=0), shift[...], preferred_element_type=jnp.float32
        )
        for u in range(SLAB):
            d = source * SLAB + u
            dx = across[u * SUB : (u + 1) * SUB, :]
            dz = volume[d + 2, here, :] - volume[d, here, :]
            dy = volume[d + 1, below, :] - volume[d + 1, above, :]
            scale = lax.rsqrt(dx * dx + dy * dy + dz * dz + 4.0)
            stage[d, 0] = SPAN + SPAN * jnp.tanh(0.5 * volume[d + 1, here, :])
            stage[d, 1] = dx * scale
            stage[d, 2] = dy * scale
            stage[d, 3] = dz * scale


def shade(flip, weights, stage, write):
    start = flip * (DEPTH - 1)
    sign = 1 - 2 * flip
    bf16 = jnp.bfloat16

    def levels(values):
        return jnp.concatenate([jnp.full((SUB, LANES), float(v), jnp.float32) for v in values], axis=0).astype(bf16)

    none = jnp.zeros((SUB, LANES), jnp.float32)
    fine_ones = jnp.full((SUB, LANES), FINE, jnp.float32)
    base = [levels((FINE * 2 * n, FINE * (2 * n + 1))) for n in range(4)]
    index = [levels((2 * n, 2 * n + 1 if n < 3 else 99)) for n in range(4)]
    zero2 = levels((0, 0))
    full2 = levels((FINE, FINE))
    ones = levels((1, 1))

    def cells(step, state):
        state = list(state)
        columns = []
        for u in range(STEP):
            at = start + sign * (step * STEP + u)
            place, nx, ny, nz = [stage[at, n] for n in range(STAGED)]
            level = jnp.floor(place)
            step_in = place - level
            floor_knot = jnp.floor(level * (1.0 / FINE))
            whole, rest, knot = pair(level, level), pair(step_in, step_in), pair(floor_knot, floor_knot)
            flat, deep, deep_full = pair(nx, ny), pair(none, nz), pair(fine_ones, nz)
            flat_top, deep_top = flat.astype(jnp.float32), deep.astype(jnp.float32)
            flat_low = pair(nx - flat_top[:SUB], ny - flat_top[SUB:])
            deep_low = pair(none, nz - deep_top[SUB:])
            ramp = [
                jnp.minimum(
                    jnp.maximum(whole - base[n], zero2 if n < 3 else deep),
                    full2 if n < 3 else deep_full,
                )
                for n in range(4)
            ]
            fine = [
                jnp.where(knot == index[n], rest, zero2 if n < 3 else deep_low) for n in range(4)
            ]
            top = ramp + [flat]
            columns.append(jnp.concatenate(top + top + fine + [flat_low, ones], axis=0))
        for two in range(STEP // 2):
            moving = jnp.concatenate(columns[2 * two : 2 * two + 2], axis=1)
            mixed = jnp.dot(weights[...], moving, preferred_element_type=jnp.float32)
            for side in range(2):
                for p in range(PASSES):
                    red, green, blue, opacity, facing = [
                        mixed[
                            (p * OUTPUTS + c) * SUB : (p * OUTPUTS + c + 1) * SUB,
                            side * LANES : (side + 1) * LANES,
                        ]
                        for c in range(OUTPUTS)
                    ]
                    bright = AMBIENT + jnp.abs(facing)
                    through = state[p * CHANNELS + 3]
                    taken = through * opacity
                    state[p * CHANNELS + 3] = through - taken
                    gain = taken * bright
                    for c, channel in enumerate((red, green, blue)):
                        state[p * CHANNELS + c] = state[p * CHANNELS + c] + gain * channel
        return tuple(state)

    zero = jnp.zeros((SUB, LANES), jnp.float32)
    one = jnp.ones((SUB, LANES), jnp.float32)
    state = cells(0, tuple([zero, zero, zero, one] * PASSES))
    for p in range(PASSES):
        for c in range(3):
            write(p, c, state[p * CHANNELS + c])
        write(p, 3, 1.0 - state[p * CHANNELS + 3])


def kernel(
    tiles,
    flips_hbm, lights_hbm, vectors_hbm, transfer_hbm, field,
    out,
    flips, lights, light_vectors, transfer,
    slab, volume, pack, left, right, halo, relay, pack_relay, draft, weights, shift, stage, image,
    table_sem, local_sem, out_sem, col_send, col_recv,
    pack_send, pack_recv, pack_far_send, pack_far_recv, pack_hop_send, pack_hop_recv,
    near_send, near_recv, far_send, far_recv, hop_send, hop_recv,
):
    rank = lax.axis_index("depth")
    tile = lax.axis_index("tile")
    ahead, behind = (rank + 1) % RANKS, (rank + RANKS - 1) % RANKS
    across = (rank + 2) % RANKS
    sides = (ahead, behind)
    east, west = (tile + 1) % tiles, (tile + tiles - 1) % tiles

    barrier = pltpu.get_barrier_semaphore()
    for where in sides:
        pl.semaphore_signal(barrier, inc=1, device_id=(where, tile), device_id_type=MESH)

    fetch = pltpu.make_async_copy(field, slab, local_sem.at[0])
    fetch.start()
    own = [
        pltpu.make_async_copy(
            field.at[:, pl.ds(pl.multiple_of(rank * ROWS + start, SUB), count), :],
            volume.at[pl.ds(1 + rank * SLAB, SLAB), pl.ds(target, count), :],
            local_sem.at[n],
        )
        for n, (start, count, target) in enumerate(
            ((0, LAST * SUB, SUB), (LAST * SUB, SUB, (LAST + 2) * SUB)), start=1
        )
    ]
    for copy in own:
        copy.start()
    tables = [
        pltpu.make_async_copy(source, target, table_sem.at[n])
        for n, (source, target) in enumerate(
            ((flips_hbm, flips), (lights_hbm, lights), (vectors_hbm, light_vectors), (transfer_hbm, transfer))
        )
    ]
    for copy in tables:
        copy.start()

    def greet():
        for where in (east, west):
            pl.semaphore_signal(barrier, inc=1, device_id=(rank, where), device_id_type=MESH)

    greet()
    pl.semaphore_wait(barrier, 4)

    def send(source, target, sent, received, side):
        return pltpu.make_async_remote_copy(
            src_ref=source,
            dst_ref=target,
            send_sem=sent,
            recv_sem=received,
            device_id=(sides[side], tile),
            device_id_type=MESH,
        )

    def near_chunk(side, c):
        return send(
            field.at[:, rows_at(sides[side] * ROWS + c * SUB), :],
            volume.at[pl.ds(1 + rank * SLAB, SLAB), pl.ds(place_of(c), SUB), :],
            near_send.at[side], near_recv.at[side, c], side,
        )

    def far_chunk(side, c):
        return send(
            field.at[pl.ds(side * HALF, HALF), rows_at(across * ROWS + c * SUB), :],
            relay.at[side, :, rows_at(c * SUB), :],
            far_send.at[side], far_recv.at[side, c], side,
        )

    def hop_chunk(side, c):
        origin = sides[1 - side]
        return send(
            relay.at[side, :, rows_at(c * SUB), :],
            volume.at[pl.ds(1 + origin * SLAB + side * HALF, HALF), pl.ds(place_of(c), SUB), :],
            hop_send.at[side], hop_recv.at[side, c], side,
        )

    def both(build, c):
        for side in range(2):
            build(side, c).start()

    def issue(order):
        for kind, c in order:
            if kind == "far":
                both(far_chunk, c)
            elif kind == "near":
                both(near_chunk, c)
            else:
                relay_on(c)

    def relay_on(c):
        for side in range(2):
            far_chunk(side, c).wait_recv()
            hop_chunk(side, c).start()

    issue(ORDER[0])

    zero_layer = jnp.zeros((TOTAL, LANES), jnp.float32)
    volume[0] = zero_layer
    volume[DEPTH + 1] = zero_layer
    fetch.wait()
    pack_borders(tile, tiles, slab, pack, left, right)

    columns = [
        pltpu.make_async_remote_copy(
            src_ref=source,
            dst_ref=pack.at[:, pl.ds(start, SUB), :],
            send_sem=col_send.at[n],
            recv_sem=col_recv.at[n],
            device_id=(rank, where),
            device_id_type=MESH,
        )
        for n, (source, start, where) in enumerate(((right, 32, east), (left, 40, west)))
    ]

    for copy in columns:
        copy.start()
    for copy in tables:
        copy.wait()
    build_weights(lights, light_vectors, transfer, draft)
    weights[...] = draft[...].astype(jnp.bfloat16)
    build_shift(shift)
    for copy in own:
        copy.wait()
    issue(ORDER[1])
    for copy in columns:
        copy.wait_recv()

    part = PACK // 2
    pack_far = [
        send(
            pack.at[across, side * part : (side + 1) * part, :],
            pack_relay.at[side],
            pack_far_send.at[side], pack_far_recv.at[side], side,
        )
        for side in range(2)
    ]
    pack_near = [
        send(pack.at[sides[side]], halo.at[rank], pack_send.at[side], pack_recv.at[side], side)
        for side in range(2)
    ]
    pack_hop = [
        send(
            pack_relay.at[side],
            halo.at[sides[1 - side], side * part : (side + 1) * part, :],
            pack_hop_send.at[side], pack_hop_recv.at[side], side,
        )
        for side in range(2)
    ]
    for copy in pack_far + pack_near:
        copy.start()
    mine = pltpu.make_async_copy(pack.at[rank], halo.at[rank], local_sem.at[3])
    mine.start()
    issue(ORDER[2])
    for side in range(2):
        pack_far[side].wait_recv()
        pack_hop[side].start()
    issue(ORDER[3])
    mine.wait()
    for side in range(2):
        pack_near[side].wait_recv()
    for side in range(2):
        pack_hop[side].wait_recv()

    for d in range(DEPTH):
        source, line = d // SLAB, d % SLAB
        volume[d + 1, 0:SUB, :] = jnp.broadcast_to(halo[source, line : line + 1, :], (SUB, LANES))
        volume[d + 1, TOTAL - SUB : TOTAL, :] = jnp.broadcast_to(
            halo[source, SLAB + line : SLAB + line + 1, :], (SUB, LANES)
        )
        volume[d + 1, ROWS : ROWS + SUB, :] = jnp.broadcast_to(
            halo[source, MIDDLE + line : MIDDLE + line + 1, :], (SUB, LANES)
        )

    flip = flips[0]

    def compute(chunk):
        prepare(chunk, volume, halo, shift, stage)

        def write(p, c, value):
            image[p, c, rows_at(chunk * SUB), :] = value

        shade(flip, weights, stage, write)
        pltpu.make_async_copy(
            image.at[:, :, rows_at(chunk * SUB), :], out.at[:, :, rows_at(chunk * SUB), :], out_sem
        ).start()

    def arrive(c):
        for side in range(2):
            near_chunk(side, c).wait_recv()
            hop_chunk(side, c).wait_recv()

    def advance(c, carry):
        @pl.when(c < CHUNKS - HOPS)
        def _():
            relay_on(c + HOPS)

        @pl.when(c < CHUNKS - NEARS)
        def _():
            both(near_chunk, c + NEARS)

        @pl.when(c < LAST)
        def _():
            arrive(c)

        @pl.when(c > 0)
        def _():
            compute(c - 1)

        @pl.when(c == LAST)
        def _():
            arrive(c)
            for d in range(DEPTH):
                volume[d + 1, ROWS + SUB - 1 : ROWS + SUB, :] = volume[d + 1, ROWS - 1 : ROWS, :]

        return carry

    lax.fori_loop(0, CHUNKS + 1, advance, 0)

    for side in range(2):
        send(
            field.at[:, pl.ds(pl.multiple_of(sides[side] * ROWS, SUB), ROWS), :],
            volume.at[pl.ds(1 + rank * SLAB, SLAB), pl.ds(SUB, ROWS), :],
            near_send.at[side], near_recv.at[side, 0], side,
        ).wait_send()
        for sent in (far_send, hop_send):
            send(
                relay.at[side], relay.at[side], sent.at[side], far_recv.at[side, 0], side
            ).wait_send()
    for copy in columns + pack_far + pack_near + pack_hop:
        copy.wait_send()
    pltpu.make_async_copy(image, out, out_sem).wait()


def solution(mesh):
    tiles = mesh.shape["tile"]

    def on_device(field, light_vectors, transfer, light_index, flips):
        anywhere = pl.BlockSpec(memory_space=pl.ANY)
        dma = pltpu.SemaphoreType.DMA
        f32, i32 = jnp.float32, jnp.int32
        return pl.pallas_call(
            functools.partial(kernel, tiles),
            out_shape=pltpu.VMEM((PASSES, CHANNELS, ROWS, LANES), f32),
            in_specs=[anywhere] * 5,
            out_specs=anywhere,
            scratch_shapes=[
                pltpu.SMEM(flips.shape, i32),
                pltpu.SMEM(light_index.shape, i32),
                pltpu.SMEM(light_vectors.shape[::-1], f32),
                pltpu.SMEM((CHANNELS, KNOTS, transfer.shape[0]), f32),
                pltpu.VMEM((SLAB, RANKS * ROWS, LANES), f32),
                pltpu.VMEM((DEPTH + 2, TOTAL, LANES), f32),
                pltpu.VMEM((RANKS, PACK, LANES), f32),
                pltpu.VMEM((RANKS, SUB, LANES), f32),
                pltpu.VMEM((RANKS, SUB, LANES), f32),
                pltpu.VMEM((RANKS, PACK, LANES), f32),
                pltpu.VMEM((2, HALF, ROWS, LANES), f32),
                pltpu.VMEM((2, PACK // 2, LANES), f32),
                pltpu.VMEM((TALL, WIDE), f32),
                pltpu.VMEM((TALL, WIDE), jnp.bfloat16),
                pltpu.VMEM((4 * LANES, LANES), jnp.bfloat16),
                pltpu.VMEM((DEPTH, STAGED, SUB, LANES), f32),
                pltpu.VMEM((PASSES, CHANNELS, ROWS, LANES), f32),
                dma((4,)), dma((4,)), dma, dma((2,)), dma((2,)),
                dma((2,)), dma((2,)), dma((2,)), dma((2,)), dma((2,)), dma((2,)),
                dma((2,)), dma((2, CHUNKS)), dma((2,)), dma((2, CHUNKS)), dma((2,)), dma((2, CHUNKS)),
            ],
            compiler_params=pltpu.CompilerParams(collective_id=0, has_side_effects=True),
            name="render",
        )(flips, light_index, light_vectors.T, jnp.transpose(transfer, (1, 2, 0)), field)

    in_specs = (P("depth", None, "tile"), P(), P(), P(), P("tile"))
    out_specs = P(None, None, "depth", "tile")
    return jax.shard_map(
        on_device, mesh=mesh, in_specs=in_specs, out_specs=out_specs, check_vma=False
    )
```

```python
import functools

import jax
import jax.numpy as jnp
from jax import lax
from jax.experimental import pallas as pl
from jax.experimental.pallas import tpu as pltpu
from jax.sharding import PartitionSpec as P

PASSES = 4
CHANNELS = 4
KNOTS = 8
AMBIENT = 0.3
RANKS = 4
SUB = 8
LANES = 128
SLAB = 16
DEPTH = 64
ROWS = 64
CHUNKS = ROWS // SUB
HALF = SLAB // 2
STEP = 64
PACK = 64
LAST = CHUNKS - 1
MIDDLE = 48
TOTAL = ROWS + 3 * SUB
TWO = 2 * SUB
FINE = 32.0
SPAN = 0.5 * (KNOTS - 1) * FINE
SLOTS = KNOTS - 1 + 3
OUTPUTS = CHANNELS + 1
WIDE = (3 * SLOTS + 2) * SUB
TALL = PASSES * OUTPUTS * SUB
STAGED = 4
ORDER = ((("far", 0), ("far", 1), ("far", 2), ("far", 3), ("far", 4), ("far", 5), ("far", 6), ("far", 7), ("near", 0), ), (("hop", 0), ("hop", 1), ), (("hop", 2), ("near", 1), ), (("near", 2), ))
HOPS = sum(kind == "hop" for part in ORDER for kind, _ in part)
NEARS = sum(kind == "near" for part in ORDER for kind, _ in part)
MESH = pl.DeviceIdType.MESH


def rows_at(start):
    return pl.ds(pl.multiple_of(start, SUB), SUB)


def place_of(chunk):
    return pl.multiple_of(SUB * (1 + chunk + chunk // LAST), SUB)


def build_weights(lights, vectors, transfer, weights):
    sub = lax.broadcasted_iota(jnp.int32, (SUB, WIDE), 0)
    lane = lax.broadcasted_iota(jnp.int32, (SUB, WIDE), 1)
    slot = lane // SUB
    diagonal = (lane % SUB) == sub
    constant = slot >= 3 * SLOTS
    item = jnp.where(constant, SLOTS, slot % SLOTS)
    is_low = ((slot >= SLOTS) & (slot < 2 * SLOTS)) | (slot == 3 * SLOTS + 1)
    for p in range(PASSES):
        chosen = lights[p]
        for c in range(OUTPUTS):
            line = jnp.zeros((SUB, WIDE), jnp.float32)
            if c < CHANNELS:
                scale = 2.0 / DEPTH if c == CHANNELS - 1 else 1.0
                values = [transfer[c, k, chosen] * scale for k in range(KNOTS)]
                for k in range(KNOTS - 1):
                    line = jnp.where(item == k, (values[k + 1] - values[k]) * (1.0 / FINE), line)
                line = jnp.where(item == SLOTS, values[0], line)
            else:
                for n, axis in enumerate((2, 0, 1)):
                    line = jnp.where(item == KNOTS - 1 + n, vectors[axis, chosen], line)
            line = jnp.where(diagonal, line, 0.0)
            high = line.astype(jnp.bfloat16).astype(jnp.float32)
            start = (p * OUTPUTS + c) * SUB
            staged = jnp.where(is_low, line - high, high)
            weights[start : start + SUB, :] = staged


def pack_borders(tile, tiles, slab, pack, left, right):
    sub = lax.broadcasted_iota(jnp.int32, (SUB, LANES), 0)
    lane = lax.broadcasted_iota(jnp.int32, (SUB, LANES), 1)
    zero = jnp.zeros((SUB, LANES), jnp.float32)

    def gather(rank, carry):
        base = rank * ROWS
        first, last = [zero] * 2, [zero] * 2
        for d in range(SLAB):
            for c in range(CHUNKS):
                place = d * CHUNKS + c
                block = slab[d, pl.ds(pl.multiple_of(base + c * SUB, SUB), SUB), :]
                here = lane == place
                first[c % 2] = jnp.where(here, pltpu.roll(block, place, 1) if place else block, first[c % 2])
                last[c % 2] = jnp.where(here, pltpu.roll(block, place + 1, 1) if place < LANES - 1 else block, last[c % 2])
        left[rank] = jnp.where(tile == 0, 0.0, first[0] + first[1])
        right[rank] = jnp.where(tile == tiles - 1, 0.0, last[0] + last[1])
        return carry

    lax.fori_loop(0, RANKS, gather, 0)
    for rank in range(RANKS):
        base = rank * ROWS
        for part in range(SLAB // SUB):
            above, below = zero, zero
            for s in range(SUB):
                d = part * SUB + s
                if rank > 0:
                    line = slab[d, base - SUB : base, :]
                    above = jnp.where(sub == s, pltpu.roll(line, (s + 1) % SUB, 0), above)
                if rank < RANKS - 1:
                    line = slab[d, base + ROWS : base + ROWS + SUB, :]
                    below = jnp.where(sub == s, pltpu.roll(line, s, 0), below)
            pack[rank, part * SUB : (part + 1) * SUB, :] = above
            pack[rank, SLAB + part * SUB : SLAB + (part + 1) * SUB, :] = below
            middle = zero
            for s in range(SUB):
                line = slab[part * SUB + s, base + LAST * SUB : base + ROWS, :]
                middle = jnp.where(sub == s, pltpu.roll(line, s, 0) if s else line, middle)
            start = MIDDLE + part * SUB
            pack[rank, start : start + SUB, :] = middle


def pair(a, b):
    return jnp.concatenate([a, b], axis=0).astype(jnp.float32).astype(jnp.bfloat16)


def build_shift(shift):
    lane = lax.broadcasted_iota(jnp.int32, (LANES, LANES), 0)
    out = lax.broadcasted_iota(jnp.int32, (LANES, LANES), 1)
    inner = jnp.where(lane == out + 1, 1.0, jnp.where(lane == out - 1, -1.0, 0.0))
    place = lane % CHUNKS
    outer = jnp.where(
        (out == LANES - 1) & (place == 0), 1.0, jnp.where((out == 0) & (place == 1), -1.0, 0.0)
    )
    for n, part in enumerate((inner, inner, outer, outer)):
        shift[n * LANES : (n + 1) * LANES, :] = part.astype(jnp.bfloat16)


def prepare(chunk, volume, halo, shift, stage):
    lane = lax.broadcasted_iota(jnp.int32, (SUB, LANES), 1)
    bf16 = jnp.bfloat16
    first = lane % CHUNKS == 0
    couple = pair(lane // 2, lane // 2)
    nothing = jnp.zeros((TWO, LANES), bf16)
    start = place_of(chunk)
    here = pl.ds(start, SUB)
    above = pl.ds(start - 1, SUB)
    below = pl.ds(start + 1, SUB)
    for source in range(RANKS):
        west = pltpu.roll(halo[source, 32:40, :], (LANES + 1 - chunk) % LANES, 1)
        east = pltpu.roll(halo[source, 40:48, :], (LANES - chunk) % LANES, 1)
        border = jnp.where(first, east, west)
        border_top = pair(border, border)
        rest = border - border_top[:SUB].astype(jnp.float32)
        border_low = pair(rest, rest)
        rows = []
        for two in range(SLAB // 2):
            d = source * SLAB + 2 * two
            x = jnp.concatenate([volume[d + 1, here, :], volume[d + 2, here, :]], axis=0)
            top = x.astype(bf16)
            low = (x - top.astype(jnp.float32)).astype(bf16)
            wanted = jnp.concatenate(
                [jnp.full((SUB, LANES), float((2 * two + n) * CHUNKS // 2), jnp.float32) for n in range(2)],
                axis=0,
            ).astype(bf16)
            mask = couple == wanted
            rows.append(
                jnp.concatenate(
                    [top, low, jnp.where(mask, border_top, nothing), jnp.where(mask, border_low, nothing)],
                    axis=1,
                )
            )
        across = jnp.dot(
            jnp.concatenate(rows, axis=0), shift[...], preferred_element_type=jnp.float32
        )
        for u in range(SLAB):
            d = source * SLAB + u
            dx = across[u * SUB : (u + 1) * SUB, :]
            dz = volume[d + 2, here, :] - volume[d, here, :]
            dy = volume[d + 1, below, :] - volume[d + 1, above, :]
            scale = lax.rsqrt(dx * dx + dy * dy + dz * dz + 4.0)
            stage[d, 0] = SPAN + SPAN * jnp.tanh(0.5 * volume[d + 1, here, :])
            stage[d, 1] = dx * scale
            stage[d, 2] = dy * scale
            stage[d, 3] = dz * scale


def shade(flip, weights, stage, write):
    start = flip * (DEPTH - 1)
    sign = 1 - 2 * flip
    bf16 = jnp.bfloat16

    def levels(values):
        return jnp.concatenate([jnp.full((SUB, LANES), float(v), jnp.float32) for v in values], axis=0).astype(bf16)

    none = jnp.zeros((SUB, LANES), jnp.float32)
    fine_ones = jnp.full((SUB, LANES), FINE, jnp.float32)
    base = [levels((FINE * 2 * n, FINE * (2 * n + 1))) for n in range(4)]
    index = [levels((2 * n, 2 * n + 1 if n < 3 else 99)) for n in range(4)]
    zero2 = levels((0, 0))
    full2 = levels((FINE, FINE))
    ones = levels((1, 1))

    def cells(step, state):
        state = list(state)
        columns = []
        for u in range(STEP):
            at = start + sign * (step * STEP + u)
            place, nx, ny, nz = [stage[at, n] for n in range(STAGED)]
            level = jnp.floor(place)
            step_in = place - level
            floor_knot = jnp.floor(level * (1.0 / FINE))
            whole, rest, knot = pair(level, level), pair(step_in, step_in), pair(floor_knot, floor_knot)
            flat, deep, deep_full = pair(nx, ny), pair(none, nz), pair(fine_ones, nz)
            flat_top, deep_top = flat.astype(jnp.float32), deep.astype(jnp.float32)
            flat_low = pair(nx - flat_top[:SUB], ny - flat_top[SUB:])
            deep_low = pair(none, nz - deep_top[SUB:])
            ramp = [
                jnp.minimum(
                    jnp.maximum(whole - base[n], zero2 if n < 3 else deep),
                    full2 if n < 3 else deep_full,
                )
                for n in range(4)
            ]
            fine = [
                jnp.where(knot == index[n], rest, zero2 if n < 3 else deep_low) for n in range(4)
            ]
            top = ramp + [flat]
            columns.append(jnp.concatenate(top + top + fine + [flat_low, ones], axis=0))
        for two in range(STEP // 2):
            moving = jnp.concatenate(columns[2 * two : 2 * two + 2], axis=1)
            mixed = jnp.dot(weights[...], moving, preferred_element_type=jnp.float32)
            for side in range(2):
                for p in range(PASSES):
                    red, green, blue, opacity, facing = [
                        mixed[
                            (p * OUTPUTS + c) * SUB : (p * OUTPUTS + c + 1) * SUB,
                            side * LANES : (side + 1) * LANES,
                        ]
                        for c in range(OUTPUTS)
                    ]
                    bright = AMBIENT + jnp.abs(facing)
                    through = state[p * CHANNELS + 3]
                    taken = through * opacity
                    state[p * CHANNELS + 3] = through - taken
                    gain = taken * bright
                    for c, channel in enumerate((red, green, blue)):
                        state[p * CHANNELS + c] = state[p * CHANNELS + c] + gain * channel
        return tuple(state)

    zero = jnp.zeros((SUB, LANES), jnp.float32)
    one = jnp.ones((SUB, LANES), jnp.float32)
    state = cells(0, tuple([zero, zero, zero, one] * PASSES))
    for p in range(PASSES):
        for c in range(3):
            write(p, c, state[p * CHANNELS + c])
        write(p, 3, 1.0 - state[p * CHANNELS + 3])


def kernel(
    tiles,
    flips_hbm, lights_hbm, vectors_hbm, transfer_hbm, field,
    out,
    flips, lights, light_vectors, transfer,
    slab, volume, pack, left, right, halo, relay, pack_relay, draft, weights, shift, stage,
    table_sem, local_sem, col_send, col_recv,
    pack_send, pack_recv, pack_far_send, pack_far_recv, pack_hop_send, pack_hop_recv,
    near_send, near_recv, far_send, far_recv, hop_send, hop_recv,
):
    rank = lax.axis_index("depth")
    tile = lax.axis_index("tile")
    ahead, behind = (rank + 1) % RANKS, (rank + RANKS - 1) % RANKS
    across = (rank + 2) % RANKS
    sides = (ahead, behind)
    east, west = (tile + 1) % tiles, (tile + tiles - 1) % tiles

    barrier = pltpu.get_barrier_semaphore()
    for where in sides:
        pl.semaphore_signal(barrier, inc=1, device_id=(where, tile), device_id_type=MESH)

    fetch = pltpu.make_async_copy(field, slab, local_sem.at[0])
    fetch.start()
    own = [
        pltpu.make_async_copy(
            field.at[:, pl.ds(pl.multiple_of(rank * ROWS + start, SUB), count), :],
            volume.at[pl.ds(1 + rank * SLAB, SLAB), pl.ds(target, count), :],
            local_sem.at[n],
        )
        for n, (start, count, target) in enumerate(
            ((0, LAST * SUB, SUB), (LAST * SUB, SUB, (LAST + 2) * SUB)), start=1
        )
    ]
    for copy in own:
        copy.start()
    tables = [
        pltpu.make_async_copy(source, target, table_sem.at[n])
        for n, (source, target) in enumerate(
            ((flips_hbm, flips), (lights_hbm, lights), (vectors_hbm, light_vectors), (transfer_hbm, transfer))
        )
    ]
    for copy in tables:
        copy.start()

    def greet():
        for where in (east, west):
            pl.semaphore_signal(barrier, inc=1, device_id=(rank, where), device_id_type=MESH)

    greet()
    pl.semaphore_wait(barrier, 4)

    def send(source, target, sent, received, side):
        return pltpu.make_async_remote_copy(
            src_ref=source,
            dst_ref=target,
            send_sem=sent,
            recv_sem=received,
            device_id=(sides[side], tile),
            device_id_type=MESH,
        )

    def near_chunk(side, c):
        return send(
            field.at[:, rows_at(sides[side] * ROWS + c * SUB), :],
            volume.at[pl.ds(1 + rank * SLAB, SLAB), pl.ds(place_of(c), SUB), :],
            near_send.at[side], near_recv.at[side, c], side,
        )

    def far_chunk(side, c):
        return send(
            field.at[pl.ds(side * HALF, HALF), rows_at(across * ROWS + c * SUB), :],
            relay.at[side, :, rows_at(c * SUB), :],
            far_send.at[side], far_recv.at[side, c], side,
        )

    def hop_chunk(side, c):
        origin = sides[1 - side]
        return send(
            relay.at[side, :, rows_at(c * SUB), :],
            volume.at[pl.ds(1 + origin * SLAB + side * HALF, HALF), pl.ds(place_of(c), SUB), :],
            hop_send.at[side], hop_recv.at[side, c], side,
        )

    def both(build, c):
        for side in range(2):
            build(side, c).start()

    def issue(order):
        for kind, c in order:
            if kind == "far":
                both(far_chunk, c)
            elif kind == "near":
                both(near_chunk, c)
            else:
                relay_on(c)

    def relay_on(c):
        for side in range(2):
            far_chunk(side, c).wait_recv()
            hop_chunk(side, c).start()

    issue(ORDER[0])

    zero_layer = jnp.zeros((TOTAL, LANES), jnp.float32)
    volume[0] = zero_layer
    volume[DEPTH + 1] = zero_layer
    fetch.wait()
    pack_borders(tile, tiles, slab, pack, left, right)

    columns = [
        pltpu.make_async_remote_copy(
            src_ref=source,
            dst_ref=pack.at[:, pl.ds(start, SUB), :],
            send_sem=col_send.at[n],
            recv_sem=col_recv.at[n],
            device_id=(rank, where),
            device_id_type=MESH,
        )
        for n, (source, start, where) in enumerate(((right, 32, east), (left, 40, west)))
    ]

    for copy in columns:
        copy.start()
    for copy in tables:
        copy.wait()
    build_weights(lights, light_vectors, transfer, draft)
    weights[...] = draft[...].astype(jnp.bfloat16)
    build_shift(shift)
    for copy in own:
        copy.wait()
    issue(ORDER[1])
    for copy in columns:
        copy.wait_recv()

    part = PACK // 2
    pack_far = [
        send(
            pack.at[across, side * part : (side + 1) * part, :],
            pack_relay.at[side],
            pack_far_send.at[side], pack_far_recv.at[side], side,
        )
        for side in range(2)
    ]
    pack_near = [
        send(pack.at[sides[side]], halo.at[rank], pack_send.at[side], pack_recv.at[side], side)
        for side in range(2)
    ]
    pack_hop = [
        send(
            pack_relay.at[side],
            halo.at[sides[1 - side], side * part : (side + 1) * part, :],
            pack_hop_send.at[side], pack_hop_recv.at[side], side,
        )
        for side in range(2)
    ]
    for copy in pack_far + pack_near:
        copy.start()
    mine = pltpu.make_async_copy(pack.at[rank], halo.at[rank], local_sem.at[3])
    mine.start()
    issue(ORDER[2])
    for side in range(2):
        pack_far[side].wait_recv()
        pack_hop[side].start()
    issue(ORDER[3])
    mine.wait()
    for side in range(2):
        pack_near[side].wait_recv()
    for side in range(2):
        pack_hop[side].wait_recv()

    for d in range(DEPTH):
        source, line = d // SLAB, d % SLAB
        volume[d + 1, 0:SUB, :] = jnp.broadcast_to(halo[source, line : line + 1, :], (SUB, LANES))
        volume[d + 1, TOTAL - SUB : TOTAL, :] = jnp.broadcast_to(
            halo[source, SLAB + line : SLAB + line + 1, :], (SUB, LANES)
        )
        volume[d + 1, ROWS : ROWS + SUB, :] = jnp.broadcast_to(
            halo[source, MIDDLE + line : MIDDLE + line + 1, :], (SUB, LANES)
        )

    flip = flips[0]

    def compute(chunk):
        prepare(chunk, volume, halo, shift, stage)

        def write(p, c, value):
            out[p, c, rows_at(chunk * SUB), :] = value

        shade(flip, weights, stage, write)

    def arrive(c):
        for side in range(2):
            near_chunk(side, c).wait_recv()
            hop_chunk(side, c).wait_recv()

    def advance(c, carry):
        @pl.when(c < CHUNKS - HOPS)
        def _():
            relay_on(c + HOPS)

        @pl.when(c < CHUNKS - NEARS)
        def _():
            both(near_chunk, c + NEARS)

        @pl.when(c < LAST)
        def _():
            arrive(c)

        @pl.when(c > 0)
        def _():
            compute(c - 1)

        @pl.when(c == LAST)
        def _():
            for d in range(DEPTH):
                volume[d + 1, ROWS + SUB - 1 : ROWS + SUB, :] = volume[d + 1, ROWS - 1 : ROWS, :]
            for side in range(2):
                send(
                    relay.at[side], relay.at[side], far_send.at[side], far_recv.at[side, 0], side
                ).wait_send()
            for copy in columns + pack_far + pack_near + pack_hop:
                copy.wait_send()
            arrive(c)

        return carry

    lax.fori_loop(0, CHUNKS + 1, advance, 0)

    for side in range(2):
        send(
            field.at[:, pl.ds(pl.multiple_of(sides[side] * ROWS, SUB), ROWS), :],
            volume.at[pl.ds(1 + rank * SLAB, SLAB), pl.ds(SUB, ROWS), :],
            near_send.at[side], near_recv.at[side, 0], side,
        ).wait_send()
        send(
            relay.at[side], relay.at[side], hop_send.at[side], far_recv.at[side, 0], side
        ).wait_send()


def solution(mesh):
    tiles = mesh.shape["tile"]

    def on_device(field, light_vectors, transfer, light_index, flips):
        anywhere = pl.BlockSpec(memory_space=pl.ANY)
        dma = pltpu.SemaphoreType.DMA
        f32, i32 = jnp.float32, jnp.int32
        return pl.pallas_call(
            functools.partial(kernel, tiles),
            out_shape=pltpu.VMEM((PASSES, CHANNELS, ROWS, LANES), f32),
            in_specs=[anywhere] * 5,
            out_specs=pl.BlockSpec(memory_space=pltpu.VMEM),
            scratch_shapes=[
                pltpu.SMEM(flips.shape, i32),
                pltpu.SMEM(light_index.shape, i32),
                pltpu.SMEM(light_vectors.shape[::-1], f32),
                pltpu.SMEM((CHANNELS, KNOTS, transfer.shape[0]), f32),
                pltpu.VMEM((SLAB, RANKS * ROWS, LANES), f32),
                pltpu.VMEM((DEPTH + 2, TOTAL, LANES), f32),
                pltpu.VMEM((RANKS, PACK, LANES), f32),
                pltpu.VMEM((RANKS, SUB, LANES), f32),
                pltpu.VMEM((RANKS, SUB, LANES), f32),
                pltpu.VMEM((RANKS, PACK, LANES), f32),
                pltpu.VMEM((2, HALF, ROWS, LANES), f32),
                pltpu.VMEM((2, PACK // 2, LANES), f32),
                pltpu.VMEM((TALL, WIDE), f32),
                pltpu.VMEM((TALL, WIDE), jnp.bfloat16),
                pltpu.VMEM((4 * LANES, LANES), jnp.bfloat16),
                pltpu.VMEM((DEPTH, STAGED, SUB, LANES), f32),
                dma((4,)), dma((4,)), dma((2,)), dma((2,)),
                dma((2,)), dma((2,)), dma((2,)), dma((2,)), dma((2,)), dma((2,)),
                dma((2,)), dma((2, CHUNKS)), dma((2,)), dma((2, CHUNKS)), dma((2,)), dma((2, CHUNKS)),
            ],
            compiler_params=pltpu.CompilerParams(collective_id=0, has_side_effects=True),
            name="render",
        )(flips, light_index, light_vectors.T, jnp.transpose(transfer, (1, 2, 0)), field)

    in_specs = (P("depth", None, "tile"), P(), P(), P(), P("tile"))
    out_specs = P(None, None, "depth", "tile")
    return jax.shard_map(
        on_device, mesh=mesh, in_specs=in_specs, out_specs=out_specs, check_vma=False
    )
```

```python
import functools

import jax
import jax.numpy as jnp
from jax import lax
from jax.experimental import pallas as pl
from jax.experimental.pallas import tpu as pltpu
from jax.sharding import PartitionSpec as P

PASSES = 4
CHANNELS = 4
KNOTS = 8
AMBIENT = 0.3
RANKS = 4
SUB = 8
LANES = 128
SLAB = 16
DEPTH = 64
ROWS = 64
CHUNKS = ROWS // SUB
HALF = SLAB // 2
INNER = SLAB - 2
OUTER = DEPTH - INNER
PACK = 64
LAST = CHUNKS - 1
MIDDLE = 48
TOTAL = ROWS + 3 * SUB
TWO = 2 * SUB
FINE = 32.0
SPAN = 0.5 * (KNOTS - 1) * FINE
SLOTS = KNOTS - 1 + 3
OUTPUTS = CHANNELS + 1
WIDE = (3 * SLOTS + 2) * SUB
TALL = PASSES * OUTPUTS * SUB
STAGED = 4
ORDER = ((("far", 0), ("far", 1), ("far", 2), ("far", 3), ("far", 4), ("far", 5), ("far", 6), ("far", 7), ("near", 0), ), (("hop", 0), ("hop", 1), ), (("hop", 2), ("near", 1), ), (("near", 2), ))
HOPS = sum(kind == "hop" for part in ORDER for kind, _ in part)
NEARS = sum(kind == "near" for part in ORDER for kind, _ in part)
MESH = pl.DeviceIdType.MESH


def rows_at(start):
    return pl.ds(pl.multiple_of(start, SUB), SUB)


def place_of(chunk):
    return pl.multiple_of(SUB * (1 + chunk + chunk // LAST), SUB)


def build_weights(lights, vectors, transfer, weights):
    sub = lax.broadcasted_iota(jnp.int32, (SUB, WIDE), 0)
    lane = lax.broadcasted_iota(jnp.int32, (SUB, WIDE), 1)
    slot = lane // SUB
    diagonal = (lane % SUB) == sub
    constant = slot >= 3 * SLOTS
    item = jnp.where(constant, SLOTS, slot % SLOTS)
    is_low = ((slot >= SLOTS) & (slot < 2 * SLOTS)) | (slot == 3 * SLOTS + 1)
    for p in range(PASSES):
        chosen = lights[p]
        for c in range(OUTPUTS):
            line = jnp.zeros((SUB, WIDE), jnp.float32)
            if c < CHANNELS:
                scale = 2.0 / DEPTH if c == CHANNELS - 1 else 1.0
                values = [transfer[c, k, chosen] * scale for k in range(KNOTS)]
                for k in range(KNOTS - 1):
                    line = jnp.where(item == k, (values[k + 1] - values[k]) * (1.0 / FINE), line)
                line = jnp.where(item == SLOTS, values[0], line)
            else:
                for n, axis in enumerate((2, 0, 1)):
                    line = jnp.where(item == KNOTS - 1 + n, vectors[axis, chosen], line)
            line = jnp.where(diagonal, line, 0.0)
            high = line.astype(jnp.bfloat16).astype(jnp.float32)
            start = (p * OUTPUTS + c) * SUB
            staged = jnp.where(is_low, line - high, high)
            weights[start : start + SUB, :] = staged


def pack_borders(tile, tiles, slab, pack, left, right):
    sub = lax.broadcasted_iota(jnp.int32, (SUB, LANES), 0)
    lane = lax.broadcasted_iota(jnp.int32, (SUB, LANES), 1)
    zero = jnp.zeros((SUB, LANES), jnp.float32)

    def gather(rank, carry):
        base = rank * ROWS
        first, last = [zero] * 2, [zero] * 2
        for d in range(SLAB):
            for c in range(CHUNKS):
                place = d * CHUNKS + c
                block = slab[d, pl.ds(pl.multiple_of(base + c * SUB, SUB), SUB), :]
                here = lane == place
                first[c % 2] = jnp.where(here, pltpu.roll(block, place, 1) if place else block, first[c % 2])
                last[c % 2] = jnp.where(here, pltpu.roll(block, place + 1, 1) if place < LANES - 1 else block, last[c % 2])
        left[rank] = jnp.where(tile == 0, 0.0, first[0] + first[1])
        right[rank] = jnp.where(tile == tiles - 1, 0.0, last[0] + last[1])
        return carry

    lax.fori_loop(0, RANKS, gather, 0)
    for rank in range(RANKS):
        base = rank * ROWS
        for part in range(SLAB // SUB):
            above, below = zero, zero
            for s in range(SUB):
                d = part * SUB + s
                if rank > 0:
                    line = slab[d, base - SUB : base, :]
                    above = jnp.where(sub == s, pltpu.roll(line, (s + 1) % SUB, 0), above)
                if rank < RANKS - 1:
                    line = slab[d, base + ROWS : base + ROWS + SUB, :]
                    below = jnp.where(sub == s, pltpu.roll(line, s, 0), below)
            pack[rank, part * SUB : (part + 1) * SUB, :] = above
            pack[rank, SLAB + part * SUB : SLAB + (part + 1) * SUB, :] = below
            middle = zero
            for s in range(SUB):
                line = slab[part * SUB + s, base + LAST * SUB : base + ROWS, :]
                middle = jnp.where(sub == s, pltpu.roll(line, s, 0) if s else line, middle)
            start = MIDDLE + part * SUB
            pack[rank, start : start + SUB, :] = middle


def pair(a, b):
    return jnp.concatenate([a, b], axis=0).astype(jnp.float32).astype(jnp.bfloat16)


def build_shift(shift):
    lane = lax.broadcasted_iota(jnp.int32, (LANES, LANES), 0)
    out = lax.broadcasted_iota(jnp.int32, (LANES, LANES), 1)
    inner = jnp.where(lane == out + 1, 1.0, jnp.where(lane == out - 1, -1.0, 0.0))
    place = lane % CHUNKS
    outer = jnp.where(
        (out == LANES - 1) & (place == 0), 1.0, jnp.where((out == 0) & (place == 1), -1.0, 0.0)
    )
    for n, part in enumerate((inner, inner, outer, outer)):
        shift[n * LANES : (n + 1) * LANES, :] = part.astype(jnp.bfloat16)


def prepare(chunk, slabs, first_layer, layers, volume, shift, stage):
    lane = lax.broadcasted_iota(jnp.int32, (SUB, LANES), 1)
    bf16 = jnp.bfloat16
    first = lane % CHUNKS == 0
    couple = pair(lane // 2, lane // 2)
    nothing = jnp.zeros((TWO, LANES), bf16)
    start = place_of(chunk)
    here = pl.ds(start, SUB)
    above = pl.ds(start - 1, SUB)
    below = pl.ds(start + 1, SUB)
    for source, halo in slabs:
        west = pltpu.roll(halo[32:40, :], (LANES + 1 - chunk) % LANES, 1)
        east = pltpu.roll(halo[40:48, :], (LANES - chunk) % LANES, 1)
        border = jnp.where(first, east, west)
        border_top = pair(border, border)
        rest = border - border_top[:SUB].astype(jnp.float32)
        border_low = pair(rest, rest)
        rows = []
        for two in range(layers // 2):
            layer = first_layer + 2 * two
            d = source * SLAB + layer
            x = jnp.concatenate([volume[d + 1, here, :], volume[d + 2, here, :]], axis=0)
            top = x.astype(bf16)
            low = (x - top.astype(jnp.float32)).astype(bf16)
            wanted = jnp.concatenate(
                [jnp.full((SUB, LANES), float((layer + n) * CHUNKS // 2), jnp.float32) for n in range(2)],
                axis=0,
            ).astype(bf16)
            mask = couple == wanted
            rows.append(
                jnp.concatenate(
                    [top, low, jnp.where(mask, border_top, nothing), jnp.where(mask, border_low, nothing)],
                    axis=1,
                )
            )
        across = jnp.dot(
            jnp.concatenate(rows, axis=0), shift[...], preferred_element_type=jnp.float32
        )
        for u in range(layers):
            d = source * SLAB + first_layer + u
            dx = across[u * SUB : (u + 1) * SUB, :]
            dz = volume[d + 2, here, :] - volume[d, here, :]
            dy = volume[d + 1, below, :] - volume[d + 1, above, :]
            scale = lax.rsqrt(dx * dx + dy * dy + dz * dz + 4.0)
            stage[d, 0] = SPAN + SPAN * jnp.tanh(0.5 * volume[d + 1, here, :])
            stage[d, 1] = dx * scale
            stage[d, 2] = dy * scale
            stage[d, 3] = dz * scale


def shade(places, weights, stage, insert):
    bf16 = jnp.bfloat16

    def levels(values):
        return jnp.concatenate([jnp.full((SUB, LANES), float(v), jnp.float32) for v in values], axis=0).astype(bf16)

    none = jnp.zeros((SUB, LANES), jnp.float32)
    fine_ones = jnp.full((SUB, LANES), FINE, jnp.float32)
    base = [levels((FINE * 2 * n, FINE * (2 * n + 1))) for n in range(4)]
    index = [levels((2 * n, 2 * n + 1 if n < 3 else 99)) for n in range(4)]
    zero2 = levels((0, 0))
    full2 = levels((FINE, FINE))
    ones = levels((1, 1))

    def cells(state):
        state = list(state)
        columns = []
        for at in places:
            place, nx, ny, nz = [stage[at, n] for n in range(STAGED)]
            level = jnp.floor(place)
            step_in = place - level
            floor_knot = jnp.floor(level * (1.0 / FINE))
            whole, rest, knot = pair(level, level), pair(step_in, step_in), pair(floor_knot, floor_knot)
            flat, deep, deep_full = pair(nx, ny), pair(none, nz), pair(fine_ones, nz)
            flat_top, deep_top = flat.astype(jnp.float32), deep.astype(jnp.float32)
            flat_low = pair(nx - flat_top[:SUB], ny - flat_top[SUB:])
            deep_low = pair(none, nz - deep_top[SUB:])
            ramp = [
                jnp.minimum(
                    jnp.maximum(whole - base[n], zero2 if n < 3 else deep),
                    full2 if n < 3 else deep_full,
                )
                for n in range(4)
            ]
            fine = [
                jnp.where(knot == index[n], rest, zero2 if n < 3 else deep_low) for n in range(4)
            ]
            top = ramp + [flat]
            columns.append(jnp.concatenate(top + top + fine + [flat_low, ones], axis=0))
        for two in range(len(places) // 2):
            moving = jnp.concatenate(columns[2 * two : 2 * two + 2], axis=1)
            mixed = jnp.dot(weights[...], moving, preferred_element_type=jnp.float32)
            for side in range(2):
                state = insert(2 * two + side, state)
                for p in range(PASSES):
                    red, green, blue, opacity, facing = [
                        mixed[
                            (p * OUTPUTS + c) * SUB : (p * OUTPUTS + c + 1) * SUB,
                            side * LANES : (side + 1) * LANES,
                        ]
                        for c in range(OUTPUTS)
                    ]
                    bright = AMBIENT + jnp.abs(facing)
                    through = state[p * CHANNELS + 3]
                    taken = through * opacity
                    state[p * CHANNELS + 3] = through - taken
                    gain = taken * bright
                    for c, channel in enumerate((red, green, blue)):
                        state[p * CHANNELS + c] = state[p * CHANNELS + c] + gain * channel
        return tuple(state)

    zero = jnp.zeros((SUB, LANES), jnp.float32)
    one = jnp.ones((SUB, LANES), jnp.float32)
    return cells([zero, zero, zero, one] * PASSES)


def kernel(
    tiles,
    flips_hbm, lights_hbm, vectors_hbm, transfer_hbm, field,
    out,
    flips, lights, light_vectors, transfer,
    slab, volume, pack, left, right, halo, relay, pack_relay, draft, weights, shift, stage, inner,
    table_sem, local_sem, col_send, col_recv,
    pack_send, pack_recv, pack_far_send, pack_far_recv, pack_hop_send, pack_hop_recv,
    near_send, near_recv, far_send, far_recv, hop_send, hop_recv,
):
    rank = lax.axis_index("depth")
    tile = lax.axis_index("tile")
    ahead, behind = (rank + 1) % RANKS, (rank + RANKS - 1) % RANKS
    across = (rank + 2) % RANKS
    sides = (ahead, behind)
    east, west = (tile + 1) % tiles, (tile + tiles - 1) % tiles

    barrier = pltpu.get_barrier_semaphore()
    for where in sides:
        pl.semaphore_signal(barrier, inc=1, device_id=(where, tile), device_id_type=MESH)

    fetch = pltpu.make_async_copy(field, slab, local_sem.at[0])
    fetch.start()
    own = [
        pltpu.make_async_copy(
            field.at[:, pl.ds(pl.multiple_of(rank * ROWS + start, SUB), count), :],
            volume.at[pl.ds(1 + rank * SLAB, SLAB), pl.ds(target, count), :],
            local_sem.at[n],
        )
        for n, (start, count, target) in enumerate(
            ((0, LAST * SUB, SUB), (LAST * SUB, SUB, (LAST + 2) * SUB)), start=1
        )
    ]
    for copy in own:
        copy.start()
    tables = [
        pltpu.make_async_copy(source, target, table_sem.at[n])
        for n, (source, target) in enumerate(
            ((flips_hbm, flips), (lights_hbm, lights), (vectors_hbm, light_vectors), (transfer_hbm, transfer))
        )
    ]
    for copy in tables:
        copy.start()

    def greet():
        for where in (east, west):
            pl.semaphore_signal(barrier, inc=1, device_id=(rank, where), device_id_type=MESH)

    greet()
    pl.semaphore_wait(barrier, 4)

    def send(source, target, sent, received, side):
        return pltpu.make_async_remote_copy(
            src_ref=source,
            dst_ref=target,
            send_sem=sent,
            recv_sem=received,
            device_id=(sides[side], tile),
            device_id_type=MESH,
        )

    def near_chunk(side, c):
        return send(
            field.at[:, rows_at(sides[side] * ROWS + c * SUB), :],
            volume.at[pl.ds(1 + rank * SLAB, SLAB), pl.ds(place_of(c), SUB), :],
            near_send.at[side], near_recv.at[side, c], side,
        )

    def far_chunk(side, c):
        return send(
            field.at[pl.ds(side * HALF, HALF), rows_at(across * ROWS + c * SUB), :],
            relay.at[side, :, rows_at(c * SUB), :],
            far_send.at[side], far_recv.at[side, c], side,
        )

    def hop_chunk(side, c):
        origin = sides[1 - side]
        return send(
            relay.at[side, :, rows_at(c * SUB), :],
            volume.at[pl.ds(1 + origin * SLAB + side * HALF, HALF), pl.ds(place_of(c), SUB), :],
            hop_send.at[side], hop_recv.at[side, c], side,
        )

    def both(build, c):
        for side in range(2):
            build(side, c).start()

    def issue(order):
        for kind, c in order:
            if kind == "far":
                both(far_chunk, c)
            elif kind == "near":
                both(near_chunk, c)
            else:
                relay_on(c)

    def relay_on(c):
        for side in range(2):
            far_chunk(side, c).wait_recv()
            hop_chunk(side, c).start()

    issue(ORDER[0])

    zero_layer = jnp.zeros((TOTAL, LANES), jnp.float32)
    volume[0] = zero_layer
    volume[DEPTH + 1] = zero_layer
    fetch.wait()
    pack_borders(tile, tiles, slab, pack, left, right)

    columns = [
        pltpu.make_async_remote_copy(
            src_ref=source,
            dst_ref=pack.at[:, pl.ds(start, SUB), :],
            send_sem=col_send.at[n],
            recv_sem=col_recv.at[n],
            device_id=(rank, where),
            device_id_type=MESH,
        )
        for n, (source, start, where) in enumerate(((right, 32, east), (left, 40, west)))
    ]

    for copy in columns:
        copy.start()
    for copy in tables:
        copy.wait()
    build_weights(lights, light_vectors, transfer, draft)
    weights[...] = draft[...].astype(jnp.bfloat16)
    build_shift(shift)
    for copy in own:
        copy.wait()
    issue(ORDER[1])
    for copy in columns:
        copy.wait_recv()

    part = PACK // 2
    pack_far = [
        send(
            pack.at[across, side * part : (side + 1) * part, :],
            pack_relay.at[side],
            pack_far_send.at[side], pack_far_recv.at[side], side,
        )
        for side in range(2)
    ]
    pack_near = [
        send(pack.at[sides[side]], halo.at[rank], pack_send.at[side], pack_recv.at[side], side)
        for side in range(2)
    ]
    pack_hop = [
        send(
            pack_relay.at[side],
            halo.at[sides[1 - side], side * part : (side + 1) * part, :],
            pack_hop_send.at[side], pack_hop_recv.at[side], side,
        )
        for side in range(2)
    ]
    for copy in pack_far + pack_near:
        copy.start()
    mine = pltpu.make_async_copy(pack.at[rank], halo.at[rank], local_sem.at[3])
    mine.start()
    issue(ORDER[2])
    flip = flips[0]
    sign = 1 - 2 * flip
    for line in range(SLAB):
        layer = 1 + rank * SLAB + line
        for start, row in ((0, line), (TOTAL - SUB, SLAB + line), (ROWS, MIDDLE + line)):
            volume[layer, start : start + SUB, :] = jnp.broadcast_to(
                pack[rank, row : row + 1, :], (SUB, LANES)
            )
    for line in range(SLAB):
        layer = 1 + rank * SLAB + line
        volume[layer, ROWS + SUB - 1 : ROWS + SUB, :] = volume[layer, ROWS - 1 : ROWS, :]

    def ahead_of_time(chunk, carry):
        prepare(chunk, [(rank, pack.at[rank])], 1, INNER, volume, shift, stage)
        places = [rank * SLAB + 1 + flip * (INNER - 1) + sign * n for n in range(INNER)]
        for n, value in enumerate(shade(places, weights, stage, lambda _, state: state)):
            inner[chunk, n] = value
        return carry

    lax.fori_loop(0, 4, ahead_of_time, 0)
    for side in range(2):
        pack_far[side].wait_recv()
        pack_hop[side].start()
    issue(ORDER[3])
    mine.wait()
    for side in range(2):
        pack_near[side].wait_recv()
    for side in range(2):
        pack_hop[side].wait_recv()

    for d in range(DEPTH):
        source, line = d // SLAB, d % SLAB
        volume[d + 1, 0:SUB, :] = jnp.broadcast_to(halo[source, line : line + 1, :], (SUB, LANES))
        volume[d + 1, TOTAL - SUB : TOTAL, :] = jnp.broadcast_to(
            halo[source, SLAB + line : SLAB + line + 1, :], (SUB, LANES)
        )
        volume[d + 1, ROWS : ROWS + SUB - 1, :] = jnp.broadcast_to(
            halo[source, MIDDLE + line : MIDDLE + line + 1, :], (SUB - 1, LANES)
        )

    hits = [
        jnp.full((SUB, LANES), jnp.where(flip == 1, RANKS - 1 - k, k), jnp.int32)
        == jnp.full((SUB, LANES), rank, jnp.int32)
        for k in range(RANKS)
    ]

    def compute(chunk):
        prepare(
            chunk, [(n, halo.at[n]) for n in range(RANKS)], 0, SLAB, volume, shift, stage
        )

        places = []
        for n in range(OUTER):
            at = flip * (OUTER - 1) + sign * n
            places.append(at + INNER * ((at + DEPTH - 1 - SLAB * rank) // DEPTH))

        def insert(n, state):
            if n % SLAB != 1:
                return state
            hit = hits[n // SLAB]
            added = []
            for p in range(PASSES):
                base = p * CHANNELS
                through = state[base + 3]
                gain = jnp.where(hit, through, 0.0)
                added += [state[base + c] + gain * inner[chunk, base + c] for c in range(3)]
                added.append(jnp.where(hit, through * inner[chunk, base + 3], through))
            return added

        state = shade(places, weights, stage, insert)
        for p in range(PASSES):
            for c in range(3):
                out[p, c, rows_at(chunk * SUB), :] = state[p * CHANNELS + c]
            out[p, 3, rows_at(chunk * SUB), :] = 1.0 - state[p * CHANNELS + 3]

    def arrive(c):
        for side in range(2):
            near_chunk(side, c).wait_recv()
            hop_chunk(side, c).wait_recv()

    def advance(c, carry):
        @pl.when(c < CHUNKS - HOPS)
        def _():
            relay_on(c + HOPS)

        @pl.when(c < CHUNKS - NEARS)
        def _():
            both(near_chunk, c + NEARS)

        @pl.when(c < CHUNKS - 4)
        def _():
            ahead_of_time(c + 4, 0)

        @pl.when(c < LAST)
        def _():
            arrive(c)

        @pl.when(c > 0)
        def _():
            compute(c - 1)

        @pl.when(c == LAST)
        def _():
            for d in range(DEPTH):
                volume[d + 1, ROWS + SUB - 1 : ROWS + SUB, :] = volume[d + 1, ROWS - 1 : ROWS, :]
            for side in range(2):
                send(
                    relay.at[side], relay.at[side], far_send.at[side], far_recv.at[side, 0], side
                ).wait_send()
            for copy in columns + pack_far + pack_near + pack_hop:
                copy.wait_send()
            arrive(c)

        return carry

    lax.fori_loop(0, CHUNKS + 1, advance, 0)

    for side in range(2):
        send(
            field.at[:, pl.ds(pl.multiple_of(sides[side] * ROWS, SUB), ROWS), :],
            volume.at[pl.ds(1 + rank * SLAB, SLAB), pl.ds(SUB, ROWS), :],
            near_send.at[side], near_recv.at[side, 0], side,
        ).wait_send()
        send(
            relay.at[side], relay.at[side], hop_send.at[side], far_recv.at[side, 0], side
        ).wait_send()


def solution(mesh):
    tiles = mesh.shape["tile"]

    def on_device(field, light_vectors, transfer, light_index, flips):
        anywhere = pl.BlockSpec(memory_space=pl.ANY)
        dma = pltpu.SemaphoreType.DMA
        f32, i32 = jnp.float32, jnp.int32
        return pl.pallas_call(
            functools.partial(kernel, tiles),
            out_shape=pltpu.VMEM((PASSES, CHANNELS, ROWS, LANES), f32),
            in_specs=[anywhere] * 5,
            out_specs=pl.BlockSpec(memory_space=pltpu.VMEM),
            scratch_shapes=[
                pltpu.SMEM(flips.shape, i32),
                pltpu.SMEM(light_index.shape, i32),
                pltpu.SMEM(light_vectors.shape[::-1], f32),
                pltpu.SMEM((CHANNELS, KNOTS, transfer.shape[0]), f32),
                pltpu.VMEM((SLAB, RANKS * ROWS, LANES), f32),
                pltpu.VMEM((DEPTH + 2, TOTAL, LANES), f32),
                pltpu.VMEM((RANKS, PACK, LANES), f32),
                pltpu.VMEM((RANKS, SUB, LANES), f32),
                pltpu.VMEM((RANKS, SUB, LANES), f32),
                pltpu.VMEM((RANKS, PACK, LANES), f32),
                pltpu.VMEM((2, HALF, ROWS, LANES), f32),
                pltpu.VMEM((2, PACK // 2, LANES), f32),
                pltpu.VMEM((TALL, WIDE), f32),
                pltpu.VMEM((TALL, WIDE), jnp.bfloat16),
                pltpu.VMEM((4 * LANES, LANES), jnp.bfloat16),
                pltpu.VMEM((DEPTH, STAGED, SUB, LANES), f32),
                pltpu.VMEM((CHUNKS, PASSES * CHANNELS, SUB, LANES), f32),
                dma((4,)), dma((4,)), dma((2,)), dma((2,)),
                dma((2,)), dma((2,)), dma((2,)), dma((2,)), dma((2,)), dma((2,)),
                dma((2,)), dma((2, CHUNKS)), dma((2,)), dma((2, CHUNKS)), dma((2,)), dma((2, CHUNKS)),
            ],
            compiler_params=pltpu.CompilerParams(collective_id=0, has_side_effects=True),
            name="render",
        )(flips, light_index, light_vectors.T, jnp.transpose(transfer, (1, 2, 0)), field)

    in_specs = (P("depth", None, "tile"), P(), P(), P(), P("tile"))
    out_specs = P(None, None, "depth", "tile")
    return jax.shard_map(
        on_device, mesh=mesh, in_specs=in_specs, out_specs=out_specs, check_vma=False
    )
```

```python
import functools

import jax
import jax.numpy as jnp
from jax import lax
from jax.experimental import pallas as pl
from jax.experimental.pallas import tpu as pltpu
from jax.sharding import PartitionSpec as P

PASSES = 4
CHANNELS = 4
KNOTS = 8
AMBIENT = 0.3
RANKS = 4
SUB = 8
LANES = 128
SLAB = 16
DEPTH = 64
ROWS = 64
CHUNKS = ROWS // SUB
HALF = SLAB // 2
INNER = SLAB - 2
OUTER = DEPTH - INNER
PACK = 64
LAST = CHUNKS - 1
MIDDLE = 48
TOTAL = ROWS + 3 * SUB
TWO = 2 * SUB
FINE = 256.0
SPAN = 0.5 * (KNOTS - 1) * FINE
SLOTS = KNOTS - 1 + 3
OUTPUTS = CHANNELS + 1
WIDE = (3 * SLOTS + 2) * SUB
TALL = PASSES * OUTPUTS * SUB
STAGED = 4
ORDER = ((("far", 0), ("far", 1), ("far", 2), ("far", 3), ("far", 4), ("far", 5), ("far", 6), ("far", 7), ("near", 0), ), (("hop", 0), ("hop", 1), ), (("hop", 2), ("near", 1), ), (("near", 2), ))
HOPS = sum(kind == "hop" for part in ORDER for kind, _ in part)
NEARS = sum(kind == "near" for part in ORDER for kind, _ in part)
MESH = pl.DeviceIdType.MESH


def rows_at(start):
    return pl.ds(pl.multiple_of(start, SUB), SUB)


def place_of(chunk):
    return pl.multiple_of(SUB * (1 + chunk + chunk // LAST), SUB)


def build_weights(lights, vectors, transfer, weights):
    sub = lax.broadcasted_iota(jnp.int32, (SUB, WIDE), 0)
    lane = lax.broadcasted_iota(jnp.int32, (SUB, WIDE), 1)
    slot = lane // SUB
    diagonal = (lane % SUB) == sub
    constant = slot >= 3 * SLOTS
    item = jnp.where(constant, SLOTS, slot % SLOTS)
    is_low = ((slot >= SLOTS) & (slot < 2 * SLOTS)) | (slot == 3 * SLOTS + 1)
    for p in range(PASSES):
        chosen = lights[p]
        for c in range(OUTPUTS):
            line = jnp.zeros((SUB, WIDE), jnp.float32)
            if c < CHANNELS:
                scale = 2.0 / DEPTH if c == CHANNELS - 1 else 1.0
                values = [transfer[c, k, chosen] * scale for k in range(KNOTS)]
                for k in range(KNOTS - 1):
                    line = jnp.where(item == k, (values[k + 1] - values[k]) * (1.0 / FINE), line)
                line = jnp.where(item == SLOTS, values[0], line)
            else:
                for n, axis in enumerate((2, 0, 1)):
                    line = jnp.where(item == KNOTS - 1 + n, vectors[axis, chosen], line)
            line = jnp.where(diagonal, line, 0.0)
            high = line.astype(jnp.bfloat16).astype(jnp.float32)
            start = (p * OUTPUTS + c) * SUB
            staged = jnp.where(is_low, line - high, high)
            weights[start : start + SUB, :] = staged


def pack_borders(tile, tiles, slab, pack, left, right):
    sub = lax.broadcasted_iota(jnp.int32, (SUB, LANES), 0)
    lane = lax.broadcasted_iota(jnp.int32, (SUB, LANES), 1)
    zero = jnp.zeros((SUB, LANES), jnp.float32)

    def gather(rank, carry):
        base = rank * ROWS
        first, last = [zero] * 2, [zero] * 2
        for d in range(SLAB):
            for c in range(CHUNKS):
                place = d * CHUNKS + c
                block = slab[d, pl.ds(pl.multiple_of(base + c * SUB, SUB), SUB), :]
                here = lane == place
                first[c % 2] = jnp.where(here, pltpu.roll(block, place, 1) if place else block, first[c % 2])
                last[c % 2] = jnp.where(here, pltpu.roll(block, place + 1, 1) if place < LANES - 1 else block, last[c % 2])
        left[rank] = jnp.where(tile == 0, 0.0, first[0] + first[1])
        right[rank] = jnp.where(tile == tiles - 1, 0.0, last[0] + last[1])
        return carry

    lax.fori_loop(0, RANKS, gather, 0)
    for rank in range(RANKS):
        base = rank * ROWS
        for part in range(SLAB // SUB):
            above, below = zero, zero
            for s in range(SUB):
                d = part * SUB + s
                if rank > 0:
                    line = slab[d, base - SUB : base, :]
                    above = jnp.where(sub == s, pltpu.roll(line, (s + 1) % SUB, 0), above)
                if rank < RANKS - 1:
                    line = slab[d, base + ROWS : base + ROWS + SUB, :]
                    below = jnp.where(sub == s, pltpu.roll(line, s, 0), below)
            pack[rank, part * SUB : (part + 1) * SUB, :] = above
            pack[rank, SLAB + part * SUB : SLAB + (part + 1) * SUB, :] = below
            middle = zero
            for s in range(SUB):
                line = slab[part * SUB + s, base + LAST * SUB : base + ROWS, :]
                middle = jnp.where(sub == s, pltpu.roll(line, s, 0) if s else line, middle)
            start = MIDDLE + part * SUB
            pack[rank, start : start + SUB, :] = middle


def pair(a, b):
    return jnp.concatenate([a, b], axis=0).astype(jnp.float32).astype(jnp.bfloat16)


def build_shift(shift):
    lane = lax.broadcasted_iota(jnp.int32, (LANES, LANES), 0)
    out = lax.broadcasted_iota(jnp.int32, (LANES, LANES), 1)
    inner = jnp.where(lane == out + 1, 1.0, jnp.where(lane == out - 1, -1.0, 0.0))
    place = lane % CHUNKS
    outer = jnp.where(
        (out == LANES - 1) & (place == 0), 1.0, jnp.where((out == 0) & (place == 1), -1.0, 0.0)
    )
    for n, part in enumerate((inner, inner, outer, outer)):
        shift[n * LANES : (n + 1) * LANES, :] = part.astype(jnp.bfloat16)


def prepare(chunk, slabs, first_layer, layers, volume, shift, stage):
    lane = lax.broadcasted_iota(jnp.int32, (SUB, LANES), 1)
    bf16 = jnp.bfloat16
    first = lane % CHUNKS == 0
    couple = pair(lane // 2, lane // 2)
    nothing = jnp.zeros((TWO, LANES), bf16)
    start = place_of(chunk)
    here = pl.ds(start, SUB)
    above = pl.ds(start - 1, SUB)
    below = pl.ds(start + 1, SUB)
    for source, halo in slabs:
        west = pltpu.roll(halo[32:40, :], (LANES + 1 - chunk) % LANES, 1)
        east = pltpu.roll(halo[40:48, :], (LANES - chunk) % LANES, 1)
        border = jnp.where(first, east, west)
        border_top = pair(border, border)
        rest = border - border_top[:SUB].astype(jnp.float32)
        border_low = pair(rest, rest)
        rows = []
        for two in range(layers // 2):
            layer = first_layer + 2 * two
            d = source * SLAB + layer
            x = jnp.concatenate([volume[d + 1, here, :], volume[d + 2, here, :]], axis=0)
            top = x.astype(bf16)
            low = (x - top.astype(jnp.float32)).astype(bf16)
            wanted = jnp.concatenate(
                [jnp.full((SUB, LANES), float((layer + n) * CHUNKS // 2), jnp.float32) for n in range(2)],
                axis=0,
            ).astype(bf16)
            mask = couple == wanted
            rows.append(
                jnp.concatenate(
                    [top, low, jnp.where(mask, border_top, nothing), jnp.where(mask, border_low, nothing)],
                    axis=1,
                )
            )
        across = jnp.dot(
            jnp.concatenate(rows, axis=0), shift[...], preferred_element_type=jnp.float32
        )
        for u in range(layers):
            d = source * SLAB + first_layer + u
            dx = across[u * SUB : (u + 1) * SUB, :]
            dz = volume[d + 2, here, :] - volume[d, here, :]
            dy = volume[d + 1, below, :] - volume[d + 1, above, :]
            scale = lax.rsqrt(dx * dx + dy * dy + dz * dz + 4.0)
            stage[d, 0] = SPAN + SPAN * jnp.tanh(0.5 * volume[d + 1, here, :])
            stage[d, 1] = dx * scale
            stage[d, 2] = dy * scale
            stage[d, 3] = dz * scale


def shade(places, weights, stage, insert):
    bf16 = jnp.bfloat16

    def levels(values):
        return jnp.concatenate([jnp.full((SUB, LANES), float(v), jnp.float32) for v in values], axis=0).astype(bf16)

    none = jnp.zeros((SUB, LANES), jnp.float32)
    index = [levels((2 * n, 2 * n + 1 if n < 3 else 99)) for n in range(4)]
    zero2 = levels((0, 0))
    full2 = levels((FINE, FINE))
    ones = levels((1, 1))

    def cells(state):
        state = list(state)
        columns = []
        for at in places:
            place, nx, ny, nz = [stage[at, n] for n in range(STAGED)]
            level = jnp.floor(place)
            step_in = place - level
            floor_knot = jnp.floor(level * (1.0 / FINE))
            within = level - floor_knot * FINE
            whole, rest, knot = pair(within, within), pair(step_in, step_in), pair(floor_knot, floor_knot)
            flat, deep = pair(nx, ny), pair(none, nz)
            flat_top, deep_top = flat.astype(jnp.float32), deep.astype(jnp.float32)
            flat_low = pair(nx - flat_top[:SUB], ny - flat_top[SUB:])
            deep_low = pair(none, nz - deep_top[SUB:])
            inside = [knot == index[n] for n in range(4)]
            ramp = [
                jnp.where(
                    inside[n], whole, jnp.where(knot > index[n], full2, zero2 if n < 3 else deep)
                )
                for n in range(4)
            ]
            fine = [jnp.where(inside[n], rest, zero2 if n < 3 else deep_low) for n in range(4)]
            top = ramp + [flat]
            columns.append(jnp.concatenate(top + top + fine + [flat_low, ones], axis=0))
        for two in range(len(places) // 2):
            moving = jnp.concatenate(columns[2 * two : 2 * two + 2], axis=1)
            mixed = jnp.dot(weights[...], moving, preferred_element_type=jnp.float32)
            for side in range(2):
                state = insert(2 * two + side, state)
                for p in range(PASSES):
                    red, green, blue, opacity, facing = [
                        mixed[
                            (p * OUTPUTS + c) * SUB : (p * OUTPUTS + c + 1) * SUB,
                            side * LANES : (side + 1) * LANES,
                        ]
                        for c in range(OUTPUTS)
                    ]
                    bright = AMBIENT + jnp.abs(facing)
                    through = state[p * CHANNELS + 3]
                    taken = through * opacity
                    state[p * CHANNELS + 3] = through - taken
                    gain = taken * bright
                    for c, channel in enumerate((red, green, blue)):
                        state[p * CHANNELS + c] = state[p * CHANNELS + c] + gain * channel
        return tuple(state)

    zero = jnp.zeros((SUB, LANES), jnp.float32)
    one = jnp.ones((SUB, LANES), jnp.float32)
    return cells([zero, zero, zero, one] * PASSES)


def kernel(
    tiles,
    flips_hbm, lights_hbm, vectors_hbm, transfer_hbm, field,
    out,
    flips, lights, light_vectors, transfer,
    slab, volume, pack, left, right, halo, relay, pack_relay, draft, weights, shift, stage, inner,
    table_sem, local_sem, col_send, col_recv,
    pack_send, pack_recv, pack_far_send, pack_far_recv, pack_hop_send, pack_hop_recv,
    near_send, near_recv, far_send, far_recv, hop_send, hop_recv,
):
    rank = lax.axis_index("depth")
    tile = lax.axis_index("tile")
    ahead, behind = (rank + 1) % RANKS, (rank + RANKS - 1) % RANKS
    across = (rank + 2) % RANKS
    sides = (ahead, behind)
    east, west = (tile + 1) % tiles, (tile + tiles - 1) % tiles

    barrier = pltpu.get_barrier_semaphore()
    for where in sides:
        pl.semaphore_signal(barrier, inc=1, device_id=(where, tile), device_id_type=MESH)

    fetch = pltpu.make_async_copy(field, slab, local_sem.at[0])
    fetch.start()
    own = [
        pltpu.make_async_copy(
            field.at[:, pl.ds(pl.multiple_of(rank * ROWS + start, SUB), count), :],
            volume.at[pl.ds(1 + rank * SLAB, SLAB), pl.ds(target, count), :],
            local_sem.at[n],
        )
        for n, (start, count, target) in enumerate(
            ((0, LAST * SUB, SUB), (LAST * SUB, SUB, (LAST + 2) * SUB)), start=1
        )
    ]
    for copy in own:
        copy.start()
    tables = [
        pltpu.make_async_copy(source, target, table_sem.at[n])
        for n, (source, target) in enumerate(
            ((flips_hbm, flips), (lights_hbm, lights), (vectors_hbm, light_vectors), (transfer_hbm, transfer))
        )
    ]
    for copy in tables:
        copy.start()

    def greet():
        for where in (east, west):
            pl.semaphore_signal(barrier, inc=1, device_id=(rank, where), device_id_type=MESH)

    greet()
    pl.semaphore_wait(barrier, 4)

    def send(source, target, sent, received, side):
        return pltpu.make_async_remote_copy(
            src_ref=source,
            dst_ref=target,
            send_sem=sent,
            recv_sem=received,
            device_id=(sides[side], tile),
            device_id_type=MESH,
        )

    def near_chunk(side, c):
        return send(
            field.at[:, rows_at(sides[side] * ROWS + c * SUB), :],
            volume.at[pl.ds(1 + rank * SLAB, SLAB), pl.ds(place_of(c), SUB), :],
            near_send.at[side], near_recv.at[side, c], side,
        )

    def far_chunk(side, c):
        return send(
            field.at[pl.ds(side * HALF, HALF), rows_at(across * ROWS + c * SUB), :],
            relay.at[side, :, rows_at(c * SUB), :],
            far_send.at[side], far_recv.at[side, c], side,
        )

    def hop_chunk(side, c):
        origin = sides[1 - side]
        return send(
            relay.at[side, :, rows_at(c * SUB), :],
            volume.at[pl.ds(1 + origin * SLAB + side * HALF, HALF), pl.ds(place_of(c), SUB), :],
            hop_send.at[side], hop_recv.at[side, c], side,
        )

    def both(build, c):
        for side in range(2):
            build(side, c).start()

    def issue(order):
        for kind, c in order:
            if kind == "far":
                both(far_chunk, c)
            elif kind == "near":
                both(near_chunk, c)
            else:
                relay_on(c)

    def relay_on(c):
        for side in range(2):
            far_chunk(side, c).wait_recv()
            hop_chunk(side, c).start()

    issue(ORDER[0])

    zero_layer = jnp.zeros((TOTAL, LANES), jnp.float32)
    volume[0] = zero_layer
    volume[DEPTH + 1] = zero_layer
    fetch.wait()
    pack_borders(tile, tiles, slab, pack, left, right)

    columns = [
        pltpu.make_async_remote_copy(
            src_ref=source,
            dst_ref=pack.at[:, pl.ds(start, SUB), :],
            send_sem=col_send.at[n],
            recv_sem=col_recv.at[n],
            device_id=(rank, where),
            device_id_type=MESH,
        )
        for n, (source, start, where) in enumerate(((right, 32, east), (left, 40, west)))
    ]

    for copy in columns:
        copy.start()
    for copy in tables:
        copy.wait()
    build_weights(lights, light_vectors, transfer, draft)
    weights[...] = draft[...].astype(jnp.bfloat16)
    build_shift(shift)
    for copy in own:
        copy.wait()
    issue(ORDER[1])
    for copy in columns:
        copy.wait_recv()

    part = PACK // 2
    pack_far = [
        send(
            pack.at[across, side * part : (side + 1) * part, :],
            pack_relay.at[side],
            pack_far_send.at[side], pack_far_recv.at[side], side,
        )
        for side in range(2)
    ]
    pack_near = [
        send(pack.at[sides[side]], halo.at[rank], pack_send.at[side], pack_recv.at[side], side)
        for side in range(2)
    ]
    pack_hop = [
        send(
            pack_relay.at[side],
            halo.at[sides[1 - side], side * part : (side + 1) * part, :],
            pack_hop_send.at[side], pack_hop_recv.at[side], side,
        )
        for side in range(2)
    ]
    for copy in pack_far + pack_near:
        copy.start()
    mine = pltpu.make_async_copy(pack.at[rank], halo.at[rank], local_sem.at[3])
    mine.start()
    issue(ORDER[2])
    flip = flips[0]
    sign = 1 - 2 * flip
    for line in range(SLAB):
        layer = 1 + rank * SLAB + line
        for start, row in ((0, line), (TOTAL - SUB, SLAB + line), (ROWS, MIDDLE + line)):
            volume[layer, start : start + SUB, :] = jnp.broadcast_to(
                pack[rank, row : row + 1, :], (SUB, LANES)
            )
    for line in range(SLAB):
        layer = 1 + rank * SLAB + line
        volume[layer, ROWS + SUB - 1 : ROWS + SUB, :] = volume[layer, ROWS - 1 : ROWS, :]

    def ahead_of_time(chunk, carry):
        prepare(chunk, [(rank, pack.at[rank])], 1, INNER, volume, shift, stage)
        places = [rank * SLAB + 1 + flip * (INNER - 1) + sign * n for n in range(INNER)]
        for n, value in enumerate(shade(places, weights, stage, lambda _, state: state)):
            inner[chunk, n] = value
        return carry

    lax.fori_loop(0, 4, ahead_of_time, 0)
    for side in range(2):
        pack_far[side].wait_recv()
        pack_hop[side].start()
    issue(ORDER[3])
    mine.wait()
    for side in range(2):
        pack_near[side].wait_recv()
    for side in range(2):
        pack_hop[side].wait_recv()

    for d in range(DEPTH):
        source, line = d // SLAB, d % SLAB
        volume[d + 1, 0:SUB, :] = jnp.broadcast_to(halo[source, line : line + 1, :], (SUB, LANES))
        volume[d + 1, TOTAL - SUB : TOTAL, :] = jnp.broadcast_to(
            halo[source, SLAB + line : SLAB + line + 1, :], (SUB, LANES)
        )
        volume[d + 1, ROWS : ROWS + SUB - 1, :] = jnp.broadcast_to(
            halo[source, MIDDLE + line : MIDDLE + line + 1, :], (SUB - 1, LANES)
        )

    hits = [
        jnp.full((SUB, LANES), jnp.where(flip == 1, RANKS - 1 - k, k), jnp.int32)
        == jnp.full((SUB, LANES), rank, jnp.int32)
        for k in range(RANKS)
    ]

    def compute(chunk):
        prepare(
            chunk, [(n, halo.at[n]) for n in range(RANKS)], 0, SLAB, volume, shift, stage
        )

        places = []
        for n in range(OUTER):
            at = flip * (OUTER - 1) + sign * n
            places.append(at + INNER * ((at + DEPTH - 1 - SLAB * rank) // DEPTH))

        def insert(n, state):
            if n % SLAB != 1:
                return state
            hit = hits[n // SLAB]
            added = []
            for p in range(PASSES):
                base = p * CHANNELS
                through = state[base + 3]
                gain = jnp.where(hit, through, 0.0)
                added += [state[base + c] + gain * inner[chunk, base + c] for c in range(3)]
                added.append(jnp.where(hit, through * inner[chunk, base + 3], through))
            return added

        state = shade(places, weights, stage, insert)
        for p in range(PASSES):
            for c in range(3):
                out[p, c, rows_at(chunk * SUB), :] = state[p * CHANNELS + c]
            out[p, 3, rows_at(chunk * SUB), :] = 1.0 - state[p * CHANNELS + 3]

    def arrive(c):
        for side in range(2):
            near_chunk(side, c).wait_recv()
            hop_chunk(side, c).wait_recv()

    def advance(c, carry):
        @pl.when(c < CHUNKS - HOPS)
        def _():
            relay_on(c + HOPS)

        @pl.when(c < CHUNKS - NEARS)
        def _():
            both(near_chunk, c + NEARS)

        @pl.when(c < CHUNKS - 4)
        def _():
            ahead_of_time(c + 4, 0)

        @pl.when(c < LAST)
        def _():
            arrive(c)

        @pl.when(c > 0)
        def _():
            compute(c - 1)

        @pl.when(c == LAST)
        def _():
            for d in range(DEPTH):
                volume[d + 1, ROWS + SUB - 1 : ROWS + SUB, :] = volume[d + 1, ROWS - 1 : ROWS, :]
            for side in range(2):
                send(
                    relay.at[side], relay.at[side], far_send.at[side], far_recv.at[side, 0], side
                ).wait_send()
            for copy in columns + pack_far + pack_near + pack_hop:
                copy.wait_send()
            arrive(c)

        return carry

    lax.fori_loop(0, CHUNKS + 1, advance, 0)

    for side in range(2):
        send(
            field.at[:, pl.ds(pl.multiple_of(sides[side] * ROWS, SUB), ROWS), :],
            volume.at[pl.ds(1 + rank * SLAB, SLAB), pl.ds(SUB, ROWS), :],
            near_send.at[side], near_recv.at[side, 0], side,
        ).wait_send()
        send(
            relay.at[side], relay.at[side], hop_send.at[side], far_recv.at[side, 0], side
        ).wait_send()


def solution(mesh):
    tiles = mesh.shape["tile"]

    def on_device(field, light_vectors, transfer, light_index, flips):
        anywhere = pl.BlockSpec(memory_space=pl.ANY)
        dma = pltpu.SemaphoreType.DMA
        f32, i32 = jnp.float32, jnp.int32
        return pl.pallas_call(
            functools.partial(kernel, tiles),
            out_shape=pltpu.VMEM((PASSES, CHANNELS, ROWS, LANES), f32),
            in_specs=[anywhere] * 5,
            out_specs=pl.BlockSpec(memory_space=pltpu.VMEM),
            scratch_shapes=[
                pltpu.SMEM(flips.shape, i32),
                pltpu.SMEM(light_index.shape, i32),
                pltpu.SMEM(light_vectors.shape[::-1], f32),
                pltpu.SMEM((CHANNELS, KNOTS, transfer.shape[0]), f32),
                pltpu.VMEM((SLAB, RANKS * ROWS, LANES), f32),
                pltpu.VMEM((DEPTH + 2, TOTAL, LANES), f32),
                pltpu.VMEM((RANKS, PACK, LANES), f32),
                pltpu.VMEM((RANKS, SUB, LANES), f32),
                pltpu.VMEM((RANKS, SUB, LANES), f32),
                pltpu.VMEM((RANKS, PACK, LANES), f32),
                pltpu.VMEM((2, HALF, ROWS, LANES), f32),
                pltpu.VMEM((2, PACK // 2, LANES), f32),
                pltpu.VMEM((TALL, WIDE), f32),
                pltpu.VMEM((TALL, WIDE), jnp.bfloat16),
                pltpu.VMEM((4 * LANES, LANES), jnp.bfloat16),
                pltpu.VMEM((DEPTH, STAGED, SUB, LANES), f32),
                pltpu.VMEM((CHUNKS, PASSES * CHANNELS, SUB, LANES), f32),
                dma((4,)), dma((4,)), dma((2,)), dma((2,)),
                dma((2,)), dma((2,)), dma((2,)), dma((2,)), dma((2,)), dma((2,)),
                dma((2,)), dma((2, CHUNKS)), dma((2,)), dma((2, CHUNKS)), dma((2,)), dma((2, CHUNKS)),
            ],
            compiler_params=pltpu.CompilerParams(collective_id=0, has_side_effects=True),
            name="render",
        )(flips, light_index, light_vectors.T, jnp.transpose(transfer, (1, 2, 0)), field)

    in_specs = (P("depth", None, "tile"), P(), P(), P(), P("tile"))
    out_specs = P(None, None, "depth", "tile")
    return jax.shard_map(
        on_device, mesh=mesh, in_specs=in_specs, out_specs=out_specs, check_vma=False
    )
```
